512 devices in a mesh: tgt: 32 (over y, x), src: 16 (over z, core).
Axes of the slice: x: 4, y: 8, z: 8, core: 2. Of those that a mesh axis runs over, the one named last changes fastest.
Arguments:
- incident: bfloat16 [128, 8, 8192], P(None, None, 'tgt'), may hold values from -6 to 6
- past_density: bfloat16 [76, 8, 8192], P(None, None, 'src'), may hold values from -6 to 6
- kernels: bfloat16 [8, 8192, 8192], P(None, 'src', 'tgt'), may hold values from -0.03125 to 0.03125
- lag_offset: int32 [32, 16, 12], P('tgt', 'src'), may hold values from 0 to 11, each once within a row
- lag_counts: int32 [32, 16], P('tgt', 'src'), may hold values from 2 to 8, as said below
- couplings: float32 [2, 8192, 256], P(None, 'tgt'), may hold values from -0.86 to 0.01
- inverse: float32 [8192, 256], P('tgt'), may hold values from -0.02 to 1.06
Outputs:
- densities: float32 [128, 8, 8192], P(None, None, 'tgt')
The draws below stay inside these ranges and needn't reach their ends.
Inputs may be any that keep to these rules, and one draw needn't show every extreme that they name: `lag_counts`: each tile has between 2 and 8 nonzero retarded lags; in every draw some tile has 8.
All inputs are finite; a program needn't handle non-finite values.
Results may differ from the reference program's by a relative error of at most 0.0014.
Values may be sent and summed in bfloat16 or wider, within the bound.
A program may use at most 64 MiB of HBM per device.

```python
import math
import jax
import jax.numpy as jnp
from jax import lax

ROW_DEV = 256
TGT_GROUPS = 32
SRC_GROUPS = 16
COL_DEV = 512
M = 8192
LOADS = 8
BLOCK_STEPS = 64
BLOCKS = 2
STEPS = 128
SLOTS = 8
LAG_SPAN = 12
HIST = 76
COUPLINGS = 2


def draw_lag_counts(key, part):
    light_key, heavy_key, spot_key = jax.random.split(jax.random.fold_in(key, 11), 3)
    light_load = jax.random.randint(light_key, (TGT_GROUPS, SRC_GROUPS), 2, 5)
    heavy_tile = jax.random.randint(heavy_key, (TGT_GROUPS, SRC_GROUPS), 0, 8) == 0
    values = jnp.where(heavy_tile, SLOTS, light_load).reshape(-1)
    chosen = jax.random.randint(spot_key, (), 0, TGT_GROUPS * SRC_GROUPS)
    values = values.at[chosen].set(SLOTS)
    return values.reshape(TGT_GROUPS, SRC_GROUPS).astype(jnp.int32)


def group_identity():
    within_group = jnp.arange(M) % ROW_DEV
    return (within_group[:, None] == jnp.arange(ROW_DEV)[None, :]).astype(jnp.float32)


def draw_couplings(key, part):
    rate_key, first_key, second_key = jax.random.split(jax.random.fold_in(key, 31), 3)
    forget = jnp.exp(jax.random.uniform(rate_key, (M,), jnp.float32, math.log(0.15), math.log(0.8)))
    retain = 1.0 - forget
    first_noise = jax.random.truncated_normal(first_key, -4.0, 4.0, (M, ROW_DEV), jnp.float32)
    second_noise = jax.random.truncated_normal(second_key, -4.0, 4.0, (M, ROW_DEV), jnp.float32)
    first = -retain[:, None] * group_identity() + 0.01 * first_noise / math.sqrt(ROW_DEV)
    second = 0.01 * second_noise / math.sqrt(ROW_DEV)
    stacked = [first, second]
    for extra in range(2, COUPLINGS):
        stacked.append(0.01 * jax.random.truncated_normal(jax.random.fold_in(second_key, extra), -4.0, 4.0, (M, ROW_DEV), jnp.float32) / math.sqrt(ROW_DEV))
    return jnp.stack(stacked[:COUPLINGS], 0)


def draw_inverse(key, part):
    noise_part = jax.random.truncated_normal(jax.random.fold_in(key, 23), -4.0, 4.0, (M, ROW_DEV), jnp.float32)
    gains = jax.random.uniform(jax.random.fold_in(key, 29), (M,), jnp.float32, 0.7, 1.05)
    return gains[:, None] * group_identity() + 0.015 * noise_part / math.sqrt(ROW_DEV)


def block_levels(stream_key, shape, cuts, least, largest):
    factor_of = 1.0
    for axis_at, parts in cuts:
        draws = jax.random.uniform(jax.random.fold_in(jax.random.fold_in(stream_key, 6), axis_at), (parts,), jnp.float32, least / len(cuts), largest / len(cuts))
        factor_of = factor_of * jnp.repeat(jnp.exp(draws), shape[axis_at] // parts).reshape((-1,) + (1,) * (len(shape) - 1 - axis_at))
    return factor_of


def noise(own_key, extent, deviation, limit, shards=(), kind=jnp.bfloat16):
    array = jax.random.normal(own_key, extent, jnp.float32) * deviation
    if len(shards) > 0:
        array = block_levels(own_key, extent, shards, -0.22, 0.18) * array
    return jnp.clip(array, min=-limit, max=limit).astype(kind)


def setup_inputs(seed: int = 0) -> dict:
    splits = jax.random.split(jax.random.key(seed), 8)
    return {
        "incident": noise(splits[0], (STEPS, LOADS, M), 1.0, 6.0, ((2, 32),)),
        "past_density": noise(splits[1], (HIST, LOADS, M), 1.0, 6.0, ((2, 16),)),
        "kernels": noise(splits[2], (SLOTS, M, M), (M * 4) ** -0.5, 0.03125, ((1, 16), (2, 32))),
        "lag_offset": jax.vmap(lambda own: jax.random.permutation(own, LAG_SPAN))(jax.random.split(splits[3], TGT_GROUPS * SRC_GROUPS)).reshape((TGT_GROUPS, SRC_GROUPS, LAG_SPAN)).astype(jnp.int32),
        "lag_counts": draw_lag_counts(jax.random.fold_in(splits[7], 71), 0),
        "couplings": draw_couplings(jax.random.fold_in(splits[7], 71), 0),
        "inverse": draw_inverse(jax.random.fold_in(splits[7], 71), 0),
    }


precise = lax.Precision.HIGHEST


def far_block(kernels, lag_offset, lag_counts, history, first_step):
    def per_target(target):
        def per_source(source, running):
            source = source.astype(jnp.int32)

            def per_slot(slot_index, partial_sum):
                slot_index = slot_index.astype(jnp.int32)
                lag_value = (BLOCK_STEPS + lag_offset[target, source, slot_index]).astype(jnp.int32)
                window = lax.dynamic_slice(history, ((first_step + HIST - lag_value).astype(jnp.int32), jnp.int32(0), (source * COL_DEV).astype(jnp.int32)), (BLOCK_STEPS, LOADS, COL_DEV))
                kernel_block = lax.dynamic_slice(kernels, (slot_index, (source * COL_DEV).astype(jnp.int32), (target * ROW_DEV).astype(jnp.int32)), (1, COL_DEV, ROW_DEV))[0]
                return partial_sum + jnp.dot(window.reshape(BLOCK_STEPS * LOADS, COL_DEV), kernel_block, preferred_element_type=jnp.float32)

            return lax.fori_loop(jnp.int32(0), lag_counts[target, source].astype(jnp.int32), per_slot, running)

        initial = jnp.zeros((BLOCK_STEPS * LOADS, ROW_DEV), jnp.float32)
        return lax.fori_loop(jnp.int32(0), jnp.int32(SRC_GROUPS), per_source, initial)

    stacked = lax.map(per_target, jnp.arange(TGT_GROUPS, dtype=jnp.int32))
    return stacked.reshape(TGT_GROUPS, BLOCK_STEPS, LOADS, ROW_DEV).transpose(1, 2, 0, 3).reshape(BLOCK_STEPS, LOADS, M)


def self_block(driving, earlier, couplings, inverse):
    grouped_couplings = couplings.reshape(COUPLINGS, TGT_GROUPS, ROW_DEV, ROW_DEV)
    grouped_inverse = inverse.reshape(TGT_GROUPS, ROW_DEV, ROW_DEV)

    def within_groups(vector_rows, matrices):
        split_rows = vector_rows.reshape(LOADS, TGT_GROUPS, ROW_DEV)
        return jnp.einsum("lgr,grk->lgk", split_rows, matrices, precision=precise).reshape(LOADS, M)

    def advance(earlier_steps, driving_step):
        adjusted = driving_step
        for shift_lag in range(1, COUPLINGS + 1):
            adjusted = adjusted - within_groups(earlier_steps[COUPLINGS - shift_lag], grouped_couplings[shift_lag - 1])
        solved = within_groups(adjusted, grouped_inverse)
        return jnp.concatenate([earlier_steps[1:], solved[None]], 0), solved

    return lax.scan(advance, earlier, driving)


def reference(incident, past_density, kernels, lag_offset, lag_counts, couplings, inverse):
    history = jnp.concatenate([past_density, jnp.zeros((STEPS, LOADS, M), jnp.bfloat16)], 0)
    earlier = past_density[HIST - COUPLINGS:].astype(jnp.float32)
    produced = []
    for block_index in range(BLOCKS):
        first_step = block_index * BLOCK_STEPS
        far_field = far_block(kernels, lag_offset, lag_counts, history, first_step)
        driving = incident[first_step:first_step + BLOCK_STEPS].astype(jnp.float32) - far_field
        earlier, solved = self_block(driving, earlier, couplings, inverse)
        produced.append(solved)
        history = history.at[HIST + first_step:HIST + first_step + BLOCK_STEPS].set(solved.astype(jnp.bfloat16))
    return jnp.concatenate(produced, 0)
```

```python
import functools

import jax
import jax.numpy as jnp
from jax import lax
from jax.experimental import pallas as pl
from jax.experimental.pallas import tpu as pltpu
from jax.sharding import PartitionSpec as P

BLOCKS = 2
LANE = 128
X = 4
MESH = pl.DeviceIdType.MESH
F32 = jnp.float32
BF16 = jnp.bfloat16

C1, C2, INV, A1, A2, Q1, Q2, Q3, D2 = range(9)


def split(value):
    hi = value.astype(BF16)
    return hi, (value - hi.astype(F32)).astype(BF16)


def dot(a, b):
    return jnp.dot(a, b, preferred_element_type=F32)


def dot3(a, b):
    return dot(a[0], b[0]) + dot(a[1], b[0]) + dot(a[0], b[1])


def kernel(
    off_ref, cnt_ref, inc_hbm, past_hbm, ker_hbm, cpl_hbm, inv_hbm, out_hbm,
    inc_v, past_v, ker_v, cpl_v, inv_v, hist, part, abuf, ssum, bsend, brecv,
    tab_hi, tab_lo, mat_hi, mat_lo, pads, shifts, drive, state, tsend, pieces, outbuf, obuf,
    load_sem, a_send, a_recv, b_send, b_recv, st_send, st_recv, t_send, p_recv,
    y_send, x_send, o_send, o_recv, f_send, out_sem,
    *, nz,
):
    slots, cols, rows = ker_v.shape
    history, loads, _ = past_v.shape
    block = inc_v.shape[0] // BLOCKS
    half = block // 2
    lead = history - block
    hrows = half * loads
    ny = nz
    t = lax.axis_index("tgt")
    s = lax.axis_index("src")
    y, x = t // X, t % X
    z, c = s // 2, s % 2
    oc = 1 - c
    member = c == x // 2
    xs_own = x % 2

    def at(y_, x_, z_, c_):
        return {"tgt": y_ * X + x_, "src": z_ * 2 + c_}

    def remote(src, dst, ssem, rsem, dev):
        return pltpu.make_async_remote_copy(
            src_ref=src, dst_ref=dst, send_sem=ssem, recv_sem=rsem,
            device_id=dev, device_id_type=MESH)

    partner = at(y, x, z, oc)

    barrier = pltpu.get_barrier_semaphore()

    def greet(dev):
        pl.semaphore_signal(barrier, inc=1, device_id=dev, device_id_type=MESH)

    for dz in range(1, nz):
        greet(at(y, x, (z + dz) % nz, c))
    greet(partner)

    @pl.when(member)
    def _():
        for core in range(2):
            greet(at(z, x, (2 * z + nz // 2 + nz - y) % nz, core))
        for dy in range(1, ny):
            greet(at((y + dy) % ny, x, z, c))

    for xs in range(2):
        @pl.when(2 * c + xs != x)
        def _():
            greet(at(y, 2 * c + xs, z, c))

    loads_list = [
        pltpu.make_async_copy(past_hbm, past_v, load_sem.at[0]),
        pltpu.make_async_copy(cpl_hbm, cpl_v, load_sem.at[1]),
        pltpu.make_async_copy(inv_hbm, inv_v, load_sem.at[2]),
        pltpu.make_async_copy(inc_hbm, inc_v, load_sem.at[3]),
    ]
    ker_loads = [
        pltpu.make_async_copy(ker_hbm.at[q], ker_v.at[q], load_sem.at[4 + q]) for q in range(slots)
    ]
    loads_list[0].start()
    for copy in ker_loads:
        copy.start()
    for copy in loads_list[1:]:
        copy.start()

    for blk in range(BLOCKS):
        hist[blk, :, history * loads:, :] = jnp.zeros((cols // LANE, block * loads, LANE), F32)
    pads[:, :half, :] = jnp.zeros((2, half, rows), F32)

    @pl.when(c == 0)
    def _():
        state[0] = jnp.zeros_like(state[0])

    tab_hi[0:rows, :] = jnp.zeros((rows, rows), BF16)
    tab_lo[0:rows, :] = jnp.zeros((rows, rows), BF16)

    loads_list[0].wait()
    for part_at in range(cols // LANE):
        lanes = slice(part_at * LANE, (part_at + 1) * LANE)
        earlier_steps = past_v[:, :, lanes].astype(F32).reshape(history * loads, LANE)
        hist[0, part_at, 0:history * loads, :] = earlier_steps
        hist[1, part_at, 0:lead * loads, :] = earlier_steps[block * loads:]

    def put(place, value):
        hi, lo = split(value)
        mat_hi[place] = hi
        mat_lo[place] = lo

    def mat(place):
        return mat_hi[place], mat_lo[place]

    loads_list[1].wait()
    loads_list[2].wait()
    put(C1, cpl_v[0])
    put(C2, cpl_v[1])
    put(INV, inv_v[...])
    for copy in ker_loads:
        copy.wait()

    def far(blk, h):
        total = None
        for q in range(slots):
            used = lax.max(lax.min(cnt_ref[0] - q, jnp.int32(1)), jnp.int32(0))
            first = history + used * (lead - history - off_ref[q]) + h * half
            place = pl.ds(first * loads, hrows)
            window = jnp.concatenate(
                [hist[blk, k, place, :].astype(BF16) for k in range(cols // LANE)], 1)
            term = dot(window, ker_v[q])
            total = term if total is None else total + term
        part[blk, pl.ds(pl.multiple_of(h * hrows, hrows), hrows), :] = total

    held = jnp.logical_and(z == y, member)

    def earlier(step):
        both = past_v[step].astype(F32)
        return jnp.where(xs_own == 0, both[:, :rows], both[:, rows:])

    last, before = split(earlier(history - 1)), split(earlier(history - 2))
    first_term = dot3(last, mat(C1)) + dot3(before, mat(C2))
    second_term = dot3(last, mat(C2))

    def far_first(h):
        far(0, h)
        keep = jnp.where(jnp.logical_and(held, h == 0), 1.0, 0.0).astype(F32)
        base = pl.multiple_of(h * hrows, hrows)
        part[0, pl.ds(base, loads), :] = part[0, pl.ds(base, loads), :] + keep * first_term
        base2 = pl.multiple_of(h * hrows + loads, loads)
        part[0, pl.ds(base2, loads), :] = part[0, pl.ds(base2, loads), :] + keep * second_term

    far_first(oc)

    @pl.when(member)
    def _():
        pl.semaphore_wait(barrier, nz + 1 + ny - 1 + X - 1)

    @pl.when(jnp.logical_not(member))
    def _():
        pl.semaphore_wait(barrier, nz + 1)

    def pair_copy(blk):
        other = pl.ds(pl.multiple_of(oc * hrows, hrows), hrows)
        return remote(part.at[blk, other], abuf.at[blk], a_send.at[blk], a_recv.at[blk], partner)

    pair_copy(0).start()
    far_first(c)

    def ring_send(blk, dz):
        there = (z + dz) % nz
        return remote(bsend.at[blk, there], brecv.at[blk, z], b_send.at[blk, dz], b_recv.at[blk, z],
                      at(y, x, there, c))

    def ring_arrival(blk, dz):
        there = (z + nz - dz) % nz
        return remote(bsend.at[blk, there], brecv.at[blk, there], b_send.at[blk, dz],
                      b_recv.at[blk, there], at(y, x, there, c))

    far_order = sorted(range(1, nz), key=lambda dz: -min(dz, nz - dz))
    near_order = sorted(range(1, nz), key=lambda dz: min(dz, nz - dz))

    def reduce_start(blk):
        pair_copy(blk).wait_recv()
        mine = pl.ds(pl.multiple_of(c * hrows, hrows), hrows)
        both = part[blk, mine, :] + abuf[blk]
        for k in range(rows // LANE):
            lanes = slice(k * LANE, (k + 1) * LANE)
            ssum[k] = both[:, lanes]
            for load in range(loads):
                bsend[blk, load, :, lanes] = ssum[k, pl.ds(load, half, stride=loads), :]
        for dz in far_order:
            ring_send(blk, dz).start()

    def reduce_finish(blk):
        total = bsend[blk, z]
        for dz in near_order:
            ring_arrival(blk, dz).wait_recv()
            total = total + brecv[blk, (z + nz - dz) % nz]
        return total

    loads_list[3].wait()
    row_at = lax.broadcasted_iota(jnp.int32, (half, hrows), 0) * loads + z
    pick = (row_at == lax.broadcasted_iota(jnp.int32, (half, hrows), 1)).astype(BF16)
    for blk in range(BLOCKS):
        steps = inc_v[pl.ds(blk * block + c * half, half)].astype(F32).reshape(hrows, rows)
        drive[blk] = dot(pick, steps.astype(BF16))

    reduce_start(0)

    def table_put(first, count, value):
        hi, lo = split(value)
        place = pl.ds(pl.multiple_of((first + 1) * rows, rows), count * rows)
        tab_hi[place, :] = hi
        tab_lo[place, :] = lo

    put(A1, -dot3(mat(C1), mat(INV)))
    put(A2, -dot3(mat(C2), mat(INV)))
    put(Q1, dot3(mat(A1), mat(A1)) + (mat_hi[A2].astype(F32) + mat_lo[A2].astype(F32)))
    put(Q2, dot3(mat(Q1), mat(A1)) + dot3(mat(A1), mat(A2)))
    put(Q3, dot3(mat(Q2), mat(A1)) + dot3(mat(Q1), mat(A2)))
    put(D2, dot3(mat(A2), mat(Q2)))
    table_put(0, 1, inv_v[...])
    table_put(1, 1, dot3(mat(INV), mat(A1)))
    table_put(2, 1, dot3(mat(INV), mat(Q1)))
    table_put(3, 1, dot3(mat(INV), mat(Q2)))

    def four_more(step, carry):
        one = pl.ds(pl.multiple_of((4 * step - 3) * rows, rows), 4 * rows)
        two = pl.ds(pl.multiple_of((4 * step - 4) * rows, rows), 4 * rows)
        value = dot3((tab_hi[one, :], tab_lo[one, :]), mat(Q3))
        value = value + dot3((tab_hi[two, :], tab_lo[two, :]), mat(D2))
        table_put(4 * step, 4, value)
        return carry

    lax.fori_loop(1, half // 4, four_more, 0)

    def state_copy(which):
        blk = which // 2
        held_by = which % 2
        return remote(outbuf.at[blk, c, z, pl.ds(half - 8, 8)], state.at[(which + 1) // 2],
                      st_send.at[which], st_recv.at[which], partner), held_by

    def state_start(which):
        copy, held_by = state_copy(which)

        @pl.when(c == held_by)
        def _():
            copy.start()

    def state_wait(which):
        copy, held_by = state_copy(which)

        @pl.when(c != held_by)
        def _():
            copy.wait_recv()

    def state_sent(which):
        copy, held_by = state_copy(which)

        @pl.when(c == held_by)
        def _():
            copy.wait_send()

    def solve(blk):
        drive[blk] = drive[blk] - reduce_finish(blk)
        if blk == 0:
            state_wait(0)
        else:
            state_wait(1)
            state_wait(2)
        from_state = split(state[blk])
        by_one, by_two = dot3(from_state, mat(C1)), dot3(from_state, mat(C2))
        row = lax.broadcasted_iota(jnp.int32, by_one.shape, 0)
        change = jnp.where(row == 0, pltpu.roll(by_one, 1, 0), 0.0)
        change = change + jnp.where(row < 2, pltpu.roll(by_two, 2, 0), 0.0)
        drive[blk, 0:8] = drive[blk, 0:8] - change
        hi, lo = split(drive[blk])
        pads[0, half:, :] = hi.astype(F32)
        pads[1, half:, :] = lo.astype(F32)
        for k in range(half):
            there = slice(k * rows, (k + 1) * rows)
            shifts[0:half, there] = pads[0, half - k:2 * half - k, :].astype(BF16)
            shifts[half:, there] = pads[1, half - k:2 * half - k, :].astype(BF16)
        both = dot(shifts[...], tab_hi[rows:, :])
        outbuf[blk, c, z] = both[:half] + both[half:] + dot(shifts[0:half, :], tab_lo[rows:, :])

    solve(0)
    state_start(0)
    state_start(1)

    def turn_copy():
        dst = pieces.at[c, xs_own, z]
        return remote(tsend, dst, t_send.at[0], p_recv.at[c, xs_own, z],
                      at((2 * y + nz // 2 + nz - z) % ny, x, y, x // 2))

    tsend[...] = outbuf[0, c, z].astype(BF16)
    turn_copy().start()

    def load_of(y_):
        return (2 * z + nz // 2 + nz - y_) % nz

    def piece(h, xs, load, ssem, dev):
        ref = pieces.at[h, xs, load]
        return remote(ref, ref, ssem, p_recv.at[h, xs, load], dev)

    def along_y(h, dy):
        return piece(h, xs_own, load_of(y), y_send.at[h, dy], at((y + dy) % ny, x, z, c))

    def along_x(h, dy, dx):
        load = load_of((y + ny - dy) % ny)
        return piece(h, xs_own, load, x_send.at[h, dy, dx], at(y, (x + dx) % X, z, c))

    def hand_on(h):
        @pl.when(member)
        def _():
            piece(h, xs_own, load_of(y), y_send.at[h, 0], partner).wait_recv()
            for dy in far_order:
                along_y(h, dy).start()
            for dx in (2, 1, 3):
                along_x(h, 0, dx).start()
            for dy in near_order:
                load = load_of((y + ny - dy) % ny)
                piece(h, xs_own, load, y_send.at[h, dy], partner).wait_recv()
                for dx in (2, 1, 3):
                    along_x(h, dy, dx).start()

    def take_in(h):
        for xs in range(2):
            @pl.when(2 * c + xs != x)
            def _():
                for load in range(loads):
                    piece(h, xs, load, x_send.at[h, 0, 0], partner).wait_recv()
        for xs in range(2):
            for load in range(loads):
                to = pl.ds((lead + h * half) * loads + load, half, stride=loads)
                for k in range(rows // LANE):
                    part_of = pieces[h, xs, load, :, k * LANE:(k + 1) * LANE]
                    hist[1, xs * (rows // LANE) + k, to, :] = part_of.astype(F32)

    def own_copy(blk, dz):
        ref = outbuf.at[blk, c, z]
        there = (z + dz) % nz
        return remote(ref, ref, o_send.at[blk, dz], o_recv.at[blk, c, z], at(y, x, there, c))

    def cross_copy(blk, h, from_z, dz):
        ref = outbuf.at[blk, h, from_z]
        return remote(ref, ref, f_send.at[blk, dz], o_recv.at[blk, h, from_z], partner)

    def spread_start(blk):
        for dz in far_order:
            own_copy(blk, dz).start()
        cross_copy(blk, c, z, 0).start()

    def spread_cross(blk):
        for dz in near_order:
            from_z = (z + nz - dz) % nz
            cross_copy(blk, c, from_z, dz).wait_recv()
            cross_copy(blk, c, from_z, dz).start()

    def spread_finish(blk):
        for dz in range(nz):
            cross_copy(blk, oc, (z + nz - dz) % nz, dz).wait_recv()

    def out_copy(blk, k):
        place = pl.ds(blk * block * loads, block * loads)
        return pltpu.make_async_copy(
            obuf.at[k, place], out_hbm.at[place, pl.ds(k * LANE, LANE)], out_sem.at[blk, k])

    def interleave(blk):
        for k in range(rows // LANE):
            for h in range(2):
                for load in range(loads):
                    to = pl.ds((blk * block + h * half) * loads + load, half, stride=loads)
                    obuf[k, to, :] = outbuf[blk, h, load, :, k * LANE:(k + 1) * LANE]
            out_copy(blk, k).start()

    hand_on(0)
    hand_on(1)
    spread_start(0)
    take_in(0)
    far(1, 0)

    @pl.when(c == 1)
    def _():
        pair_copy(1).start()

    @pl.when(c == 0)
    def _():
        reduce_start(1)

    take_in(1)
    far(1, 1)

    @pl.when(c == 0)
    def _():
        pair_copy(1).start()

    @pl.when(c == 1)
    def _():
        reduce_start(1)

    spread_cross(0)
    spread_finish(0)
    interleave(0)

    solve(1)
    state_start(2)
    spread_start(1)
    spread_cross(1)
    spread_finish(1)
    interleave(1)

    for blk in range(BLOCKS):
        pair_copy(blk).wait_send()
        for dz in range(1, nz):
            ring_send(blk, dz).wait_send()
            own_copy(blk, dz).wait_send()
        for dz in range(nz):
            cross_copy(blk, c, (z + nz - dz) % nz, dz).wait_send()
        for k in range(rows // LANE):
            out_copy(blk, k).wait()
    for which in range(3):
        state_sent(which)
    turn_copy().wait_send()

    @pl.when(member)
    def _():
        for h in range(2):
            for dy in range(1, ny):
                along_y(h, dy).wait_send()
            for dy in range(ny):
                for dx in range(1, X):
                    along_x(h, dy, dx).wait_send()


def local(nz, incident, past_density, kernels, lag_offset, lag_counts, couplings, inverse):
    steps, loads, rows = incident.shape
    history, _, cols = past_density.shape
    slots = kernels.shape[0]
    block = steps // BLOCKS
    half = block // 2
    hrows = half * loads
    vmem = pltpu.VMEM
    dma = pltpu.SemaphoreType.DMA
    out = pl.pallas_call(
        functools.partial(kernel, nz=nz),
        out_shape=jax.ShapeDtypeStruct((steps * loads, rows), F32),
        in_specs=[pl.BlockSpec(memory_space=pltpu.SMEM)] * 2
        + [pl.BlockSpec(memory_space=pl.ANY)] * 5,
        out_specs=pl.BlockSpec(memory_space=pl.ANY),
        scratch_shapes=[
            vmem((steps, loads, rows), BF16),
            vmem((history, loads, cols), BF16),
            vmem((slots, cols, rows), BF16),
            vmem((2, rows, rows), F32),
            vmem((rows, rows), F32),
            vmem((BLOCKS, cols // LANE, (history + block) * loads, LANE), F32),
            vmem((BLOCKS, block * loads, rows), F32),
            vmem((BLOCKS, hrows, rows), F32),
            vmem((rows // LANE, hrows, LANE), F32),
            vmem((BLOCKS, nz, half, rows), F32),
            vmem((BLOCKS, nz, half, rows), F32),
            vmem(((half + 1) * rows, rows), BF16),
            vmem(((half + 1) * rows, rows), BF16),
            vmem((9, rows, rows), BF16),
            vmem((9, rows, rows), BF16),
            vmem((2, 2 * half, rows), F32),
            vmem((2 * half, half * rows), BF16),
            vmem((BLOCKS, half, rows), F32),
            vmem((2, 8, rows), F32),
            vmem((half, rows), BF16),
            vmem((2, 2, loads, half, rows), BF16),
            vmem((BLOCKS, 2, nz, half, rows), F32),
            vmem((rows // LANE, steps * loads, LANE), F32),
            dma((4 + slots,)),
            dma((BLOCKS,)),
            dma((BLOCKS,)),
            dma((BLOCKS, nz)),
            dma((BLOCKS, nz)),
            dma((3,)),
            dma((3,)),
            dma((1,)),
            dma((2, 2, loads)),
            dma((2, nz)),
            dma((2, nz, X)),
            dma((BLOCKS, nz)),
            dma((BLOCKS, 2, nz)),
            dma((BLOCKS, nz)),
            dma((BLOCKS, rows // LANE)),
        ],
        compiler_params=pltpu.CompilerParams(
            collective_id=0, has_side_effects=True, vmem_limit_bytes=60 * 1024 * 1024),
    )(
        lag_offset.reshape(-1), lag_counts.reshape(-1),
        incident, past_density, kernels, couplings, inverse,
    )
    return out.reshape(steps, loads, rows)


def solution(mesh):
    return jax.shard_map(
        functools.partial(local, mesh.shape["src"] // 2),
        mesh=mesh,
        in_specs=(
            P(None, None, "tgt"),
            P(None, None, "src"),
            P(None, "src", "tgt"),
            P("tgt", "src", None),
            P("tgt", "src"),
            P(None, "tgt", None),
            P("tgt", None),
        ),
        out_specs=P(None, None, "tgt"),
        check_vma=False,
    )
```

```python
import functools

import jax
import jax.numpy as jnp
from jax import lax
from jax.experimental import pallas as pl
from jax.experimental.pallas import tpu as pltpu
from jax.sharding import PartitionSpec as P

BLOCKS = 2
LANE = 128
X = 4
MESH = pl.DeviceIdType.MESH
F32 = jnp.float32
BF16 = jnp.bfloat16

C1, C2, INV, A1, A2, Q1, Q2, Q3, D2 = range(9)


def split(value):
    hi = value.astype(BF16)
    return hi, (value - hi.astype(F32)).astype(BF16)


def dot(a, b):
    return jnp.dot(a, b, preferred_element_type=F32)


def dot3(a, b):
    return dot(a[0], b[0]) + dot(a[1], b[0]) + dot(a[0], b[1])


def kernel(
    off_ref, cnt_ref, inc_hbm, past_hbm, ker_hbm, cpl_hbm, inv_hbm, out_hbm,
    inc_v, past_v, ker_v, cpl_v, inv_v, hist, part, abuf, ssum, bsend, brecv,
    tab_hi, tab_lo, mat_hi, mat_lo, pads, shifts, drive, state, tsend, pieces, outbuf, obuf,
    load_sem, a_send, a_recv, b_send, b_recv, st_send, st_recv, t_send, p_recv,
    px_recv, early_recv, r_send, y_send, x_send, o_send, o_recv, f_send, f_recv, out_sem,
    *, nz,
):
    slots, cols, rows = ker_v.shape
    history, loads, _ = past_v.shape
    block = inc_v.shape[0] // BLOCKS
    half = block // 2
    lead = history - block
    hrows = half * loads
    ny = nz
    t = lax.axis_index("tgt")
    s = lax.axis_index("src")
    y, x = t // X, t % X
    z, c = s // 2, s % 2
    oc = 1 - c
    member = c == x // 2
    xs_own = x % 2

    def at(y_, x_, z_, c_):
        return {"tgt": y_ * X + x_, "src": z_ * 2 + c_}

    def remote(src, dst, ssem, rsem, dev):
        return pltpu.make_async_remote_copy(
            src_ref=src, dst_ref=dst, send_sem=ssem, recv_sem=rsem,
            device_id=dev, device_id_type=MESH)

    partner = at(y, x, z, oc)

    past_load = pltpu.make_async_copy(past_hbm, past_v, load_sem.at[0])
    cpl_load = pltpu.make_async_copy(cpl_hbm, cpl_v, load_sem.at[1])
    inv_load = pltpu.make_async_copy(inv_hbm, inv_v, load_sem.at[2])
    inc_load = pltpu.make_async_copy(inc_hbm, inc_v, load_sem.at[3])
    past_load.start()
    for q in range(slots):
        pltpu.make_async_copy(ker_hbm.at[q], ker_v.at[q], load_sem.at[4]).start()
    ker_load = pltpu.make_async_copy(ker_hbm, ker_v, load_sem.at[4])

    barrier = pltpu.get_barrier_semaphore()

    def greet(dev):
        pl.semaphore_signal(barrier, inc=1, device_id=dev, device_id_type=MESH)

    for dz in range(1, nz):
        greet(at(y, x, (z + dz) % nz, c))
    greet(partner)

    @pl.when(member)
    def _():
        for core in range(2):
            greet(at(z, x, (2 * z + nz // 2 + nz - y) % nz, core))
        for dy in range(1, ny):
            greet(at((y + dy) % ny, x, z, c))

    for xs in range(2):
        @pl.when(2 * c + xs != x)
        def _():
            greet(at(y, 2 * c + xs, z, c))

        @pl.when((x + 2) % X == 2 * c + xs)
        def _():
            greet(at(y, (x + 1) % X, z, c))

    hist[0, :, history * loads:, :] = jnp.zeros((cols // LANE, block * loads, LANE), F32)

    past_load.wait()
    for copy in (cpl_load, inv_load, inc_load):
        copy.start()
    for part_at in range(cols // LANE):
        lanes = slice(part_at * LANE, (part_at + 1) * LANE)
        hist[0, part_at, 0:history * loads, :] = (
            past_v[:, :, lanes].astype(F32).reshape(history * loads, LANE))

    def put(place, value):
        hi, lo = split(value)
        mat_hi[place] = hi
        mat_lo[place] = lo

    def mat(place):
        return mat_hi[place], mat_lo[place]

    cpl_load.wait()
    inv_load.wait()
    put(C1, cpl_v[0])
    put(C2, cpl_v[1])
    put(INV, inv_v[...])
    ker_load.wait()

    def far(blk, h):
        windows = []
        for q in range(slots):
            used = lax.max(lax.min(cnt_ref[0] - q, jnp.int32(1)), jnp.int32(0))
            first = history + used * (lead - history - off_ref[q]) + h * half
            place = pl.ds(first * loads, hrows)
            windows += [hist[blk, k, place, :].astype(BF16) for k in range(cols // LANE)]
        part[blk, pl.ds(pl.multiple_of(h * hrows, hrows), hrows), :] = dot(
            jnp.concatenate(windows, 1), ker_v[...].reshape(slots * cols, rows))

    def far_whole(h):
        @pl.when(t >= 0)
        def _():
            far(1, h)

    held = jnp.logical_and(z == y, member)

    def earlier(step):
        both = past_v[step].astype(F32)
        return jnp.where(xs_own == 0, both[:, :rows], both[:, rows:])

    last, before = split(earlier(history - 1)), split(earlier(history - 2))
    first_term = dot3(last, mat(C1)) + dot3(before, mat(C2))
    second_term = dot3(last, mat(C2))

    def far_first(h):
        @pl.when(t >= 0)
        def _():
            far(0, h)

        keep = jnp.where(jnp.logical_and(held, h == 0), 1.0, 0.0).astype(F32)
        base = pl.multiple_of(h * hrows, hrows)
        part[0, pl.ds(base, loads), :] = part[0, pl.ds(base, loads), :] + keep * first_term
        base2 = pl.multiple_of(h * hrows + loads, loads)
        part[0, pl.ds(base2, loads), :] = part[0, pl.ds(base2, loads), :] + keep * second_term

    far_first(oc)

    relayer = jnp.logical_or((x + 1) % X == 2 * c, (x + 1) % X == 2 * c + 1)
    peers = nz + 1 + jnp.where(member, ny - 1 + X - 1, 0) + jnp.where(relayer, 1, 0)
    pl.semaphore_wait(barrier, peers)

    def pair_copy(blk):
        other = pl.ds(pl.multiple_of(oc * hrows, hrows), hrows)
        return remote(part.at[blk, other], abuf.at[blk], a_send.at[blk], a_recv.at[blk], partner)

    pair_copy(0).start()
    far_first(c)

    def ring_send(blk, dz):
        there = (z + dz) % nz
        return remote(bsend.at[blk, there], brecv.at[blk, z], b_send.at[blk], b_recv.at[blk],
                      at(y, x, there, c))

    def ring_all(blk):
        every = pl.ds(0, nz - 1)
        return remote(bsend.at[blk, every], brecv.at[blk, every], b_send.at[blk], b_recv.at[blk],
                      partner)

    far_order = sorted(range(1, nz), key=lambda dz: -min(dz, nz - dz))
    near_order = sorted(range(1, nz), key=lambda dz: min(dz, nz - dz))

    def reduce_start(blk):
        pair_copy(blk).wait_recv()
        mine = pl.ds(pl.multiple_of(c * hrows, hrows), hrows)
        both = part[blk, mine, :] + abuf[blk]
        for k in range(rows // LANE):
            lanes = slice(k * LANE, (k + 1) * LANE)
            ssum[k] = both[:, lanes]
            for load in range(loads):
                bsend[blk, load, :, lanes] = ssum[k, pl.ds(load, half, stride=loads), :]
        for dz in far_order:
            ring_send(blk, dz).start()

    def reduce_finish(blk):
        total = bsend[blk, z]
        ring_all(blk).wait_recv()
        for dz in range(1, nz):
            total = total + brecv[blk, (z + dz) % nz]
        return total

    inc_load.wait()
    row_at = lax.broadcasted_iota(jnp.int32, (half, hrows), 0) * loads + z
    pick = (row_at == lax.broadcasted_iota(jnp.int32, (half, hrows), 1)).astype(BF16)
    for blk in range(BLOCKS):
        steps = inc_v[pl.ds(blk * block + c * half, half)].astype(F32).reshape(hrows, rows)
        drive[blk] = dot(pick, steps.astype(BF16))

    reduce_start(0)

    hist[1, :, history * loads:, :] = jnp.zeros((cols // LANE, block * loads, LANE), F32)
    hist[1, :, 0:lead * loads, :] = hist[0, :, block * loads:history * loads, :]
    pads[:, :half, :] = jnp.zeros((2, half, rows), F32)

    tab_hi[0:rows, :] = jnp.zeros((rows, rows), BF16)
    tab_lo[0:rows, :] = jnp.zeros((rows, rows), BF16)

    def table_put(first, count, value):
        hi, lo = split(value)
        place = pl.ds(pl.multiple_of((first + 1) * rows, rows), count * rows)
        tab_hi[place, :] = hi
        tab_lo[place, :] = lo

    put(A1, -dot3(mat(C1), mat(INV)))
    put(A2, -dot3(mat(C2), mat(INV)))
    put(Q1, dot3(mat(A1), mat(A1)) + (mat_hi[A2].astype(F32) + mat_lo[A2].astype(F32)))
    put(Q2, dot3(mat(Q1), mat(A1)) + dot3(mat(A1), mat(A2)))
    put(Q3, dot3(mat(Q2), mat(A1)) + dot3(mat(Q1), mat(A2)))
    put(D2, dot3(mat(A2), mat(Q2)))
    table_put(0, 1, inv_v[...])
    table_put(1, 1, dot3(mat(INV), mat(A1)))
    table_put(2, 1, dot3(mat(INV), mat(Q1)))
    table_put(3, 1, dot3(mat(INV), mat(Q2)))

    def four_more(step, carry):
        one = pl.ds(pl.multiple_of((4 * step - 3) * rows, rows), 4 * rows)
        two = pl.ds(pl.multiple_of((4 * step - 4) * rows, rows), 4 * rows)
        value = dot3((tab_hi[one, :], tab_lo[one, :]), mat(Q3))
        value = value + dot3((tab_hi[two, :], tab_lo[two, :]), mat(D2))
        table_put(4 * step, 4, value)
        return carry

    lax.fori_loop(1, half // 4, four_more, 0)

    def state_copy(which):
        blk = which // 2
        held_by = which % 2
        return remote(outbuf.at[blk, c, z, pl.ds(half - 8, 8)], state.at[(which + 1) // 2],
                      st_send.at[which], st_recv.at[which], partner), held_by

    def state_start(which):
        copy, held_by = state_copy(which)

        @pl.when(c == held_by)
        def _():
            copy.start()

    def state_wait(which):
        copy, held_by = state_copy(which)

        @pl.when(c != held_by)
        def _():
            copy.wait_recv()

    def state_sent(which):
        copy, held_by = state_copy(which)

        @pl.when(c == held_by)
        def _():
            copy.wait_send()

    def respond(blk, from_state):
        from_state = split(from_state)
        by_one, by_two = dot3(from_state, mat(C1)), dot3(from_state, mat(C2))
        row = lax.broadcasted_iota(jnp.int32, by_one.shape, 0)
        change = jnp.where(row == 0, pltpu.roll(by_one, 1, 0), 0.0)
        change = change + jnp.where(row < 2, pltpu.roll(by_two, 2, 0), 0.0)
        drive[blk, 0:8] = drive[blk, 0:8] - change
        hi, lo = split(drive[blk])
        pads[0, half:, :] = hi.astype(F32)
        pads[1, half:, :] = lo.astype(F32)
        for k in range(half):
            there = slice(k * rows, (k + 1) * rows)
            shifts[0:half, there] = pads[0, half - k:2 * half - k, :].astype(BF16)
            shifts[half:, there] = pads[1, half - k:2 * half - k, :].astype(BF16)
        both = dot(shifts[...], tab_hi[rows:, :])
        outbuf[blk, c, z] = both[:half] + both[half:] + dot(shifts[0:half, :], tab_lo[rows:, :])

    drive[0] = drive[0] - reduce_finish(0)

    @pl.when(c == 0)
    def _():
        respond(0, jnp.zeros((8, rows), F32))

    @pl.when(c == 1)
    def _():
        state_wait(0)
        respond(0, state[0])

    state_start(0)
    state_start(1)

    def turn_copy():
        dst = pieces.at[c, xs_own, z]
        return remote(tsend, dst, t_send.at[0], p_recv.at[c, z],
                      at((2 * y + nz // 2 + nz - z) % ny, x, y, x // 2))

    tsend[...] = outbuf[0, c, z].astype(BF16)
    turn_copy().start()

    def load_of(y_):
        return (2 * z + nz // 2 + nz - y_) % nz

    def arrived(h, load):
        ref = pieces.at[h, xs_own, load]
        remote(ref, ref, t_send.at[0], p_recv.at[h, load], partner).wait_recv()

    def along_y(h, dy):
        load = load_of(y)
        ref = pieces.at[h, xs_own, load]
        return remote(ref, ref, y_send.at[h], p_recv.at[h, load], at((y + dy) % ny, x, z, c))

    def along_x(h, dy, dx):
        ref = pieces.at[h, xs_own, load_of((y + ny - dy) % ny)]
        return remote(ref, ref, x_send.at[h, dx - 1], px_recv.at[h, xs_own],
                      at(y, (x + dx) % X, z, c))

    def all_x(h, xs, dx):
        ref = pieces.at[h, xs]
        return remote(ref, ref, x_send.at[h, dx - 1], px_recv.at[h, xs], partner)

    y_order = [0] + near_order
    by_left, direct = y_order[:ny // 2], y_order[ny // 2:]

    def early(h, xs, dy, dev):
        load = load_of((y + ny - dy) % ny)
        ref = pieces.at[h, xs, load]
        return remote(ref, ref, r_send.at[h], early_recv.at[h, dy], dev)

    def to_left(h, dy):
        load = load_of((y + ny - dy) % ny)
        ref = pieces.at[h, xs_own, load]
        return remote(ref, ref, x_send.at[h, X - 2], early_recv.at[h, dy],
                      at(y, (x + X - 1) % X, z, c))

    def relays(h):
        for xs in range(2):
            @pl.when((x + 1) % X == 2 * c + xs)
            def _():
                for dy in by_left:
                    early(h, xs, dy, partner).wait_recv()
                    early_on(h, xs, dy).start()

    def early_on(h, xs, dy):
        load = load_of((y + ny - dy) % ny)
        ref = pieces.at[h, xs, load]
        return remote(ref, ref, r_send.at[h], px_recv.at[h, xs], at(y, (x + X - 1) % X, z, c))

    def handed_on(h):
        some = pieces.at[h, 0, pl.ds(0, ny - 1)]
        remote(some, some, y_send.at[h], p_recv.at[h, 0], partner).wait_send()
        all_x(h, 0, 1).wait_send()
        all_x(h, 0, 3).wait_send()
        later = pieces.at[h, 0, pl.ds(0, len(direct))]
        remote(later, later, x_send.at[h, 1], p_recv.at[h, 0], partner).wait_send()

    def hand_on(h):
        @pl.when(member)
        def _():
            arrived(h, load_of(y))
            for dy in far_order:
                along_y(h, dy).start()
            for dy in y_order:
                if dy > 0:
                    arrived(h, load_of((y + ny - dy) % ny))
                if dy in by_left:
                    to_left(h, dy).start()
                    along_x(h, dy, 1).start()
                else:
                    for dx in (2, 1, 3):
                        along_x(h, dy, dx).start()

    def take_in(h):
        for xs in range(2):
            delta = (x + X - 2 * c - xs) % X

            @pl.when(jnp.logical_or(delta == 1, delta == 2))
            def _():
                all_x(h, xs, 1).wait_recv()

            @pl.when(delta == 3)
            def _():
                later = pieces.at[h, xs, pl.ds(0, len(direct))]
                remote(later, later, r_send.at[h], px_recv.at[h, xs], partner).wait_recv()
        for xs in range(2):
            for load in range(loads):
                to = pl.ds((lead + h * half) * loads + load, half, stride=loads)
                for k in range(rows // LANE):
                    part_of = pieces[h, xs, load, :, k * LANE:(k + 1) * LANE]
                    hist[1, xs * (rows // LANE) + k, to, :] = part_of.astype(F32)

    def direct_sem(blk, from_z):
        return o_recv.at[0] if blk == 0 else o_recv.at[1 + from_z]

    def own_copy(blk, dz):
        ref = outbuf.at[blk, c, z]
        there = (z + dz) % nz
        return remote(ref, ref, o_send.at[blk], direct_sem(blk, z), at(y, x, there, c))

    def own_all(blk):
        some = outbuf.at[blk, c, pl.ds(0, nz - 1)]
        return remote(some, some, o_send.at[blk], o_recv.at[0], partner)

    def own_arrival(blk, from_z):
        ref = outbuf.at[blk, c, from_z]
        remote(ref, ref, o_send.at[blk], direct_sem(blk, from_z), partner).wait_recv()

    def cross_copy(blk, from_z):
        ref = outbuf.at[blk, c, from_z]
        return remote(ref, ref, f_send.at[blk], f_recv.at[blk], partner)

    def cross_all(blk, h):
        ref = outbuf.at[blk, h]
        return remote(ref, ref, f_send.at[blk], f_recv.at[blk], partner)

    def spread_start(blk):
        for dz in far_order:
            own_copy(blk, dz).start()
        cross_copy(blk, z).start()

    def spread_cross(blk):
        if blk == 0:
            own_all(blk).wait_recv()
        for dz in near_order:
            from_z = (z + nz - dz) % nz
            if blk == 1:
                own_arrival(blk, from_z)
            cross_copy(blk, from_z).start()

    def spread_sent(blk):
        own_all(blk).wait_send()
        cross_all(blk, 0).wait_send()

    def out_copy(blk, h, k):
        first = pl.multiple_of((blk * block + h * half) * loads, loads)
        place = pl.ds(first, hrows)
        return pltpu.make_async_copy(
            obuf.at[k, place], out_hbm.at[place, pl.ds(k * LANE, LANE)], out_sem.at[blk, h, k])

    def out_start(blk, h):
        for k in range(rows // LANE):
            for load in range(loads):
                to = pl.ds((blk * block + h * half) * loads + load, half, stride=loads)
                obuf[k, to, :] = outbuf[blk, h, load, :, k * LANE:(k + 1) * LANE]
            out_copy(blk, h, k).start()

    hand_on(0)
    relays(0)
    hand_on(1)
    relays(1)
    spread_start(0)
    take_in(0)
    far_whole(0)

    @pl.when(c == 1)
    def _():
        pair_copy(1).start()

    @pl.when(c == 0)
    def _():
        reduce_start(1)

    take_in(1)
    far_whole(1)

    @pl.when(c == 0)
    def _():
        pair_copy(1).start()

    @pl.when(c == 1)
    def _():
        reduce_start(1)

    spread_cross(0)
    ring_all(0).wait_send()
    for blk in range(BLOCKS):
        pair_copy(blk).wait_send()
    turn_copy().wait_send()
    for which in range(2):
        state_sent(which)

    @pl.when(member)
    def _():
        for h in range(2):
            handed_on(h)

    @pl.when(relayer)
    def _():
        for h in range(2):
            some = pieces.at[h, 0, pl.ds(0, len(by_left))]
            remote(some, some, r_send.at[h], px_recv.at[h, 0], partner).wait_send()

    drive[1] = drive[1] - reduce_finish(1)
    state_wait(1)
    state_wait(2)

    @pl.when(t >= 0)
    def _():
        respond(1, state[1])

    spread_start(1)
    state_start(2)

    cross_all(0, oc).wait_recv()
    spread_sent(0)
    ring_all(1).wait_send()
    for h in range(2):
        out_start(0, h)
    state_sent(2)

    spread_cross(1)

    @pl.when(c == 1)
    def _():
        cross_all(1, 0).wait_recv()
        out_start(1, 0)
        out_start(1, 1)

    @pl.when(c == 0)
    def _():
        out_start(1, 0)
        cross_all(1, 1).wait_recv()
        out_start(1, 1)

    spread_sent(1)
    for k in range(rows // LANE):
        for blk in range(BLOCKS):
            for h in range(2):
                out_copy(blk, h, k).wait()


def local(nz, incident, past_density, kernels, lag_offset, lag_counts, couplings, inverse):
    steps, loads, rows = incident.shape
    history, _, cols = past_density.shape
    slots = kernels.shape[0]
    block = steps // BLOCKS
    half = block // 2
    hrows = half * loads
    vmem = pltpu.VMEM
    dma = pltpu.SemaphoreType.DMA
    out = pl.pallas_call(
        functools.partial(kernel, nz=nz),
        out_shape=jax.ShapeDtypeStruct((steps * loads, rows), F32),
        in_specs=[pl.BlockSpec(memory_space=pltpu.SMEM)] * 2
        + [pl.BlockSpec(memory_space=pl.ANY)] * 5,
        out_specs=pl.BlockSpec(memory_space=pl.ANY),
        scratch_shapes=[
            vmem((steps, loads, rows), BF16),
            vmem((history, loads, cols), BF16),
            vmem((slots, cols, rows), BF16),
            vmem((2, rows, rows), F32),
            vmem((rows, rows), F32),
            vmem((BLOCKS, cols // LANE, (history + block) * loads, LANE), F32),
            vmem((BLOCKS, block * loads, rows), F32),
            vmem((BLOCKS, hrows, rows), F32),
            vmem((rows // LANE, hrows, LANE), F32),
            vmem((BLOCKS, nz, half, rows), F32),
            vmem((BLOCKS, nz, half, rows), F32),
            vmem(((half + 1) * rows, rows), BF16),
            vmem(((half + 1) * rows, rows), BF16),
            vmem((9, rows, rows), BF16),
            vmem((9, rows, rows), BF16),
            vmem((2, 2 * half, rows), F32),
            vmem((2 * half, half * rows), BF16),
            vmem((BLOCKS, half, rows), F32),
            vmem((2, 8, rows), F32),
            vmem((half, rows), BF16),
            vmem((2, 2, loads, half, rows), BF16),
            vmem((BLOCKS, 2, nz, half, rows), F32),
            vmem((rows // LANE, steps * loads, LANE), F32),
            dma((5,)),
            dma((BLOCKS,)),
            dma((BLOCKS,)),
            dma((BLOCKS,)),
            dma((BLOCKS,)),
            dma((3,)),
            dma((3,)),
            dma((1,)),
            dma((2, loads)),
            dma((2, 2)),
            dma((2, nz)),
            dma((2,)),
            dma((2,)),
            dma((2, X - 1)),
            dma((BLOCKS,)),
            dma((1 + nz,)),
            dma((BLOCKS,)),
            dma((BLOCKS,)),
            dma((BLOCKS, 2, rows // LANE)),
        ],
        compiler_params=pltpu.CompilerParams(
            collective_id=0, has_side_effects=True, vmem_limit_bytes=60 * 1024 * 1024),
    )(
        lag_offset.reshape(-1), lag_counts.reshape(-1),
        incident, past_density, kernels, couplings, inverse,
    )
    return out.reshape(steps, loads, rows)


def solution(mesh):
    return jax.shard_map(
        functools.partial(local, mesh.shape["src"] // 2),
        mesh=mesh,
        in_specs=(
            P(None, None, "tgt"),
            P(None, None, "src"),
            P(None, "src", "tgt"),
            P("tgt", "src", None),
            P("tgt", "src"),
            P(None, "tgt", None),
            P("tgt", None),
        ),
        out_specs=P(None, None, "tgt"),
        check_vma=False,
    )
```

```python
import functools

import jax
import jax.numpy as jnp
from jax import lax
from jax.experimental import pallas as pl
from jax.experimental.pallas import tpu as pltpu
from jax.sharding import PartitionSpec as P

BLOCKS = 2
LANE = 128
X = 4
MESH = pl.DeviceIdType.MESH
F32 = jnp.float32
BF16 = jnp.bfloat16

C1, C2, INV, A1, A2, Q1, Q2, Q3, D2 = range(9)


def split(value):
    hi = value.astype(BF16)
    return hi, (value - hi.astype(F32)).astype(BF16)


def dot(a, b):
    return jnp.dot(a, b, preferred_element_type=F32)


def dot3(a, b):
    return dot(a[0], b[0]) + dot(a[1], b[0]) + dot(a[0], b[1])


def kernel(
    off_ref, cnt_ref, inc_hbm, past_hbm, ker_hbm, cpl_hbm, inv_hbm, out_hbm,
    inc_v, past_v, ker_v, cpl_v, inv_v, hist, part, abuf, ssum, bsend, brecv,
    tab_hi, tab_lo, mat_hi, mat_lo, pads, shifts, drive, state, tsend, pieces, outbuf, obuf,
    load_sem, a_send, a_recv, b_send, b_recv, st_send, st_recv, t_send, p_recv,
    px_recv, y_send, x_send, o_send, o_recv, f_send, f_recv, out_sem,
    *, nz,
):
    slots, cols, rows = ker_v.shape
    history, loads, _ = past_v.shape
    block = inc_v.shape[0] // BLOCKS
    half = block // 2
    lead = history - block
    hrows = half * loads
    ny = nz
    t = lax.axis_index("tgt")
    s = lax.axis_index("src")
    y, x = t // X, t % X
    z, c = s // 2, s % 2
    oc = 1 - c
    member = c == x // 2
    xs_own = x % 2

    def at(y_, x_, z_, c_):
        return {"tgt": y_ * X + x_, "src": z_ * 2 + c_}

    def remote(src, dst, ssem, rsem, dev):
        return pltpu.make_async_remote_copy(
            src_ref=src, dst_ref=dst, send_sem=ssem, recv_sem=rsem,
            device_id=dev, device_id_type=MESH)

    partner = at(y, x, z, oc)

    past_load = pltpu.make_async_copy(past_hbm, past_v, load_sem.at[0])
    cpl_load = pltpu.make_async_copy(cpl_hbm, cpl_v, load_sem.at[1])
    inv_load = pltpu.make_async_copy(inv_hbm, inv_v, load_sem.at[2])
    inc_load = pltpu.make_async_copy(inc_hbm, inc_v, load_sem.at[3])
    past_load.start()
    for q in range(slots):
        pltpu.make_async_copy(ker_hbm.at[q], ker_v.at[q], load_sem.at[4]).start()
    ker_load = pltpu.make_async_copy(ker_hbm, ker_v, load_sem.at[4])
    for copy in (cpl_load, inv_load, inc_load):
        copy.start()

    barrier = pltpu.get_barrier_semaphore()

    def greet(dev):
        pl.semaphore_signal(barrier, inc=1, device_id=dev, device_id_type=MESH)

    for dz in range(1, nz):
        greet(at(y, x, (z + dz) % nz, c))
    greet(partner)

    @pl.when(member)
    def _():
        for core in range(2):
            greet(at(z, x, (2 * z + nz // 2 + nz - y) % nz, core))
        for dy in range(1, ny):
            greet(at((y + dy) % ny, x, z, c))

    for xs in range(2):
        @pl.when(2 * c + xs != x)
        def _():
            greet(at(y, 2 * c + xs, z, c))

    hist[0, :, history * loads:, :] = jnp.zeros((cols // LANE, block * loads, LANE), F32)

    past_load.wait()
    @pl.when(t >= 0)
    def _():
        for part_at in range(cols // LANE):
            lanes = slice(part_at * LANE, (part_at + 1) * LANE)
            hist[0, part_at, 0:history * loads, :] = (
                past_v[:, :, lanes].astype(F32).reshape(history * loads, LANE))

    def put(place, value):
        hi, lo = split(value)
        mat_hi[place] = hi
        mat_lo[place] = lo

    def mat(place):
        return mat_hi[place], mat_lo[place]

    cpl_load.wait()
    inv_load.wait()
    put(C1, cpl_v[0])
    put(C2, cpl_v[1])
    put(INV, inv_v[...])
    ker_load.wait()

    def far(blk, h):
        windows = []
        for q in range(slots):
            used = lax.max(lax.min(cnt_ref[0] - q, jnp.int32(1)), jnp.int32(0))
            first = history + used * (lead - history - off_ref[q]) + h * half
            place = pl.ds(first * loads, hrows)
            windows += [hist[blk, k, place, :].astype(BF16) for k in range(cols // LANE)]
        part[blk, pl.ds(pl.multiple_of(h * hrows, hrows), hrows), :] = dot(
            jnp.concatenate(windows, 1), ker_v[...].reshape(slots * cols, rows))

    def far_whole(h):
        @pl.when(t >= 0)
        def _():
            far(1, h)

    held = jnp.logical_and(z == y, member)

    def earlier(step):
        both = past_v[step].astype(F32)
        return jnp.where(xs_own == 0, both[:, :rows], both[:, rows:])

    last, before = split(earlier(history - 1)), split(earlier(history - 2))
    first_term = dot3(last, mat(C1)) + dot3(before, mat(C2))
    second_term = dot3(last, mat(C2))

    def far_first(h):
        @pl.when(t >= 0)
        def _():
            far(0, h)

        keep = jnp.where(jnp.logical_and(held, h == 0), 1.0, 0.0).astype(F32)
        base = pl.multiple_of(h * hrows, hrows)
        part[0, pl.ds(base, loads), :] = part[0, pl.ds(base, loads), :] + keep * first_term
        base2 = pl.multiple_of(h * hrows + loads, loads)
        part[0, pl.ds(base2, loads), :] = part[0, pl.ds(base2, loads), :] + keep * second_term

    far_first(oc)

    @pl.when(member)
    def _():
        pl.semaphore_wait(barrier, nz + 1 + ny - 1 + X - 1)

    @pl.when(jnp.logical_not(member))
    def _():
        pl.semaphore_wait(barrier, nz + 1)

    def pair_copy(blk):
        other = pl.ds(pl.multiple_of(oc * hrows, hrows), hrows)
        return remote(part.at[blk, other], abuf.at[blk], a_send.at[blk], a_recv.at[blk], partner)

    pair_copy(0).start()
    far_first(c)

    def ring_send(blk, dz):
        there = (z + dz) % nz
        return remote(bsend.at[blk, there], brecv.at[blk, z], b_send.at[blk], b_recv.at[blk],
                      at(y, x, there, c))

    def ring_all(blk):
        every = pl.ds(0, nz - 1)
        return remote(bsend.at[blk, every], brecv.at[blk, every], b_send.at[blk], b_recv.at[blk],
                      partner)

    far_order = sorted(range(1, nz), key=lambda dz: -min(dz, nz - dz))
    near_order = sorted(range(1, nz), key=lambda dz: min(dz, nz - dz))

    def reduce_start(blk):
        pair_copy(blk).wait_recv()
        mine = pl.ds(pl.multiple_of(c * hrows, hrows), hrows)
        both = part[blk, mine, :] + abuf[blk]
        for k in range(rows // LANE):
            lanes = slice(k * LANE, (k + 1) * LANE)
            ssum[k] = both[:, lanes]
            for load in range(loads):
                bsend[blk, load, :, lanes] = ssum[k, pl.ds(load, half, stride=loads), :]
        for dz in far_order:
            ring_send(blk, dz).start()

    def reduce_finish(blk):
        total = bsend[blk, z]
        ring_all(blk).wait_recv()
        for dz in range(1, nz):
            total = total + brecv[blk, (z + dz) % nz]
        return total

    inc_load.wait()
    row_at = lax.broadcasted_iota(jnp.int32, (half, hrows), 0) * loads + z
    pick = (row_at == lax.broadcasted_iota(jnp.int32, (half, hrows), 1)).astype(BF16)
    for blk in range(BLOCKS):
        steps = inc_v[pl.ds(blk * block + c * half, half)].astype(F32).reshape(hrows, rows)
        drive[blk] = dot(pick, steps.astype(BF16))

    reduce_start(0)

    hist[1, :, history * loads:, :] = jnp.zeros((cols // LANE, block * loads, LANE), F32)
    hist[1, :, 0:lead * loads, :] = hist[0, :, block * loads:history * loads, :]
    pads[:, :half, :] = jnp.zeros((2, half, rows), F32)

    tab_hi[0:rows, :] = jnp.zeros((rows, rows), BF16)
    tab_lo[0:rows, :] = jnp.zeros((rows, rows), BF16)

    def table_put(first, count, value):
        hi, lo = split(value)
        place = pl.ds(pl.multiple_of((first + 1) * rows, rows), count * rows)
        tab_hi[place, :] = hi
        tab_lo[place, :] = lo

    @pl.when(t >= 0)
    def _():
        put(A1, -dot3(mat(C1), mat(INV)))
        put(A2, -dot3(mat(C2), mat(INV)))
        put(Q1, dot3(mat(A1), mat(A1)) + (mat_hi[A2].astype(F32) + mat_lo[A2].astype(F32)))
        put(Q2, dot3(mat(Q1), mat(A1)) + dot3(mat(A1), mat(A2)))
        put(Q3, dot3(mat(Q2), mat(A1)) + dot3(mat(Q1), mat(A2)))
        put(D2, dot3(mat(A2), mat(Q2)))
        table_put(0, 1, inv_v[...])
        table_put(1, 1, dot3(mat(INV), mat(A1)))
        table_put(2, 1, dot3(mat(INV), mat(Q1)))
        table_put(3, 1, dot3(mat(INV), mat(Q2)))

    def four_more(step, carry):
        one = pl.ds(pl.multiple_of((4 * step - 3) * rows, rows), 4 * rows)
        two = pl.ds(pl.multiple_of((4 * step - 4) * rows, rows), 4 * rows)
        value = dot3((tab_hi[one, :], tab_lo[one, :]), mat(Q3))
        value = value + dot3((tab_hi[two, :], tab_lo[two, :]), mat(D2))
        table_put(4 * step, 4, value)
        return carry

    @pl.when(t >= 0)
    def _():
        lax.fori_loop(1, half // 4, four_more, 0)

    def state_copy(which):
        blk = which // 2
        held_by = which % 2
        return remote(outbuf.at[blk, c, z, pl.ds(half - 8, 8)], state.at[(which + 1) // 2],
                      st_send.at[which], st_recv.at[which], partner), held_by

    def state_start(which):
        copy, held_by = state_copy(which)

        @pl.when(c == held_by)
        def _():
            copy.start()

    def state_wait(which):
        copy, held_by = state_copy(which)

        @pl.when(c != held_by)
        def _():
            copy.wait_recv()

    def state_sent(which):
        copy, held_by = state_copy(which)

        @pl.when(c == held_by)
        def _():
            copy.wait_send()

    def respond(blk, from_state):
        from_state = split(from_state)
        by_one, by_two = dot3(from_state, mat(C1)), dot3(from_state, mat(C2))
        row = lax.broadcasted_iota(jnp.int32, by_one.shape, 0)
        change = jnp.where(row == 0, pltpu.roll(by_one, 1, 0), 0.0)
        change = change + jnp.where(row < 2, pltpu.roll(by_two, 2, 0), 0.0)
        drive[blk, 0:8] = drive[blk, 0:8] - change
        hi, lo = split(drive[blk])
        pads[0, half:, :] = hi.astype(F32)
        pads[1, half:, :] = lo.astype(F32)
        for k in range(half):
            there = slice(k * rows, (k + 1) * rows)
            shifts[0:half, there] = pads[0, half - k:2 * half - k, :].astype(BF16)
            shifts[half:, there] = pads[1, half - k:2 * half - k, :].astype(BF16)
        both = dot(shifts[...], tab_hi[rows:, :])
        outbuf[blk, c, z] = both[:half] + both[half:] + dot(shifts[0:half, :], tab_lo[rows:, :])

    drive[0] = drive[0] - reduce_finish(0)

    @pl.when(c == 0)
    def _():
        respond(0, jnp.zeros((8, rows), F32))

    @pl.when(c == 1)
    def _():
        state_wait(0)
        respond(0, state[0])

    state_start(0)
    state_start(1)

    def turn_copy():
        dst = pieces.at[c, xs_own, z]
        return remote(tsend, dst, t_send.at[0], p_recv.at[c, z],
                      at((2 * y + nz // 2 + nz - z) % ny, x, y, x // 2))

    tsend[...] = outbuf[0, c, z].astype(BF16)
    turn_copy().start()

    def load_of(y_):
        return (2 * z + nz // 2 + nz - y_) % nz

    def arrived(h, load):
        ref = pieces.at[h, xs_own, load]
        remote(ref, ref, t_send.at[0], p_recv.at[h, load], partner).wait_recv()

    def along_y(h, dy):
        load = load_of(y)
        ref = pieces.at[h, xs_own, load]
        return remote(ref, ref, y_send.at[h], p_recv.at[h, load], at((y + dy) % ny, x, z, c))

    def along_x(h, dy, dx):
        ref = pieces.at[h, xs_own, load_of((y + ny - dy) % ny)]
        return remote(ref, ref, x_send.at[h, dx - 1], px_recv.at[h, xs_own],
                      at(y, (x + dx) % X, z, c))

    def all_x(h, xs, dx):
        ref = pieces.at[h, xs]
        return remote(ref, ref, x_send.at[h, dx - 1], px_recv.at[h, xs], partner)

    def handed_on(h):
        some = pieces.at[h, 0, pl.ds(0, ny - 1)]
        remote(some, some, y_send.at[h], p_recv.at[h, 0], partner).wait_send()
        for dx in range(1, X):
            all_x(h, 0, dx).wait_send()

    def hand_on(h):
        @pl.when(member)
        def _():
            arrived(h, load_of(y))
            for dy in far_order:
                along_y(h, dy).start()
            for dx in (2, 1, 3):
                along_x(h, 0, dx).start()
            for dy in near_order:
                arrived(h, load_of((y + ny - dy) % ny))
                for dx in (2, 1, 3):
                    along_x(h, dy, dx).start()

    def take_in(h):
        for xs in range(2):
            @pl.when(2 * c + xs != x)
            def _():
                all_x(h, xs, 1).wait_recv()
        for xs in range(2):
            for load in range(loads):
                to = pl.ds((lead + h * half) * loads + load, half, stride=loads)
                for k in range(rows // LANE):
                    part_of = pieces[h, xs, load, :, k * LANE:(k + 1) * LANE]
                    hist[1, xs * (rows // LANE) + k, to, :] = part_of.astype(F32)

    def direct_sem(blk, from_z):
        return o_recv.at[0] if blk == 0 else o_recv.at[1 + from_z]

    def own_copy(blk, dz):
        ref = outbuf.at[blk, c, z]
        there = (z + dz) % nz
        return remote(ref, ref, o_send.at[blk], direct_sem(blk, z), at(y, x, there, c))

    def own_all(blk):
        some = outbuf.at[blk, c, pl.ds(0, nz - 1)]
        return remote(some, some, o_send.at[blk], o_recv.at[0], partner)

    def own_arrival(blk, from_z):
        ref = outbuf.at[blk, c, from_z]
        remote(ref, ref, o_send.at[blk], direct_sem(blk, from_z), partner).wait_recv()

    def cross_copy(blk, from_z):
        ref = outbuf.at[blk, c, from_z]
        return remote(ref, ref, f_send.at[blk], f_recv.at[blk], partner)

    def cross_all(blk, h):
        ref = outbuf.at[blk, h]
        return remote(ref, ref, f_send.at[blk], f_recv.at[blk], partner)

    def spread_start(blk):
        for dz in far_order:
            own_copy(blk, dz).start()
        cross_copy(blk, z).start()

    def spread_cross(blk):
        if blk == 0:
            own_all(blk).wait_recv()
        for dz in near_order:
            from_z = (z + nz - dz) % nz
            if blk == 1:
                own_arrival(blk, from_z)
            cross_copy(blk, from_z).start()

    def spread_sent(blk):
        own_all(blk).wait_send()
        cross_all(blk, 0).wait_send()

    def out_copy(blk, h, k):
        first = pl.multiple_of((blk * block + h * half) * loads, loads)
        place = pl.ds(first, hrows)
        return pltpu.make_async_copy(
            obuf.at[k, place], out_hbm.at[place, pl.ds(k * LANE, LANE)], out_sem.at[blk, h, k])

    def out_start(blk, h):
        for k in range(rows // LANE):
            for load in range(loads):
                to = pl.ds((blk * block + h * half) * loads + load, half, stride=loads)
                obuf[k, to, :] = outbuf[blk, h, load, :, k * LANE:(k + 1) * LANE]
            out_copy(blk, h, k).start()

    hand_on(0)
    hand_on(1)
    spread_start(0)
    take_in(0)
    far_whole(0)

    @pl.when(c == 1)
    def _():
        pair_copy(1).start()

    @pl.when(c == 0)
    def _():
        reduce_start(1)

    take_in(1)
    far_whole(1)

    @pl.when(c == 0)
    def _():
        pair_copy(1).start()

    @pl.when(c == 1)
    def _():
        reduce_start(1)

    spread_cross(0)
    ring_all(0).wait_send()
    for blk in range(BLOCKS):
        pair_copy(blk).wait_send()
    turn_copy().wait_send()
    for which in range(2):
        state_sent(which)

    @pl.when(member)
    def _():
        for h in range(2):
            handed_on(h)

    drive[1] = drive[1] - reduce_finish(1)
    state_wait(1)
    state_wait(2)

    @pl.when(t >= 0)
    def _():
        respond(1, state[1])

    spread_start(1)
    state_start(2)

    cross_all(0, oc).wait_recv()
    spread_sent(0)
    ring_all(1).wait_send()
    for h in range(2):
        out_start(0, h)
    state_sent(2)

    spread_cross(1)

    @pl.when(c == 1)
    def _():
        cross_all(1, 0).wait_recv()
        out_start(1, 0)
        out_start(1, 1)

    @pl.when(c == 0)
    def _():
        out_start(1, 0)
        cross_all(1, 1).wait_recv()
        out_start(1, 1)

    spread_sent(1)
    for k in range(rows // LANE):
        for blk in range(BLOCKS):
            for h in range(2):
                out_copy(blk, h, k).wait()


def local(nz, incident, past_density, kernels, lag_offset, lag_counts, couplings, inverse):
    steps, loads, rows = incident.shape
    history, _, cols = past_density.shape
    slots = kernels.shape[0]
    block = steps // BLOCKS
    half = block // 2
    hrows = half * loads
    vmem = pltpu.VMEM
    dma = pltpu.SemaphoreType.DMA
    out = pl.pallas_call(
        functools.partial(kernel, nz=nz),
        out_shape=jax.ShapeDtypeStruct((steps * loads, rows), F32),
        in_specs=[pl.BlockSpec(memory_space=pltpu.SMEM)] * 2
        + [pl.BlockSpec(memory_space=pl.ANY)] * 5,
        out_specs=pl.BlockSpec(memory_space=pl.ANY),
        scratch_shapes=[
            vmem((steps, loads, rows), BF16),
            vmem((history, loads, cols), BF16),
            vmem((slots, cols, rows), BF16),
            vmem((2, rows, rows), F32),
            vmem((rows, rows), F32),
            vmem((BLOCKS, cols // LANE, (history + block) * loads, LANE), F32),
            vmem((BLOCKS, block * loads, rows), F32),
            vmem((BLOCKS, hrows, rows), F32),
            vmem((rows // LANE, hrows, LANE), F32),
            vmem((BLOCKS, nz, half, rows), F32),
            vmem((BLOCKS, nz, half, rows), F32),
            vmem(((half + 1) * rows, rows), BF16),
            vmem(((half + 1) * rows, rows), BF16),
            vmem((9, rows, rows), BF16),
            vmem((9, rows, rows), BF16),
            vmem((2, 2 * half, rows), F32),
            vmem((2 * half, half * rows), BF16),
            vmem((BLOCKS, half, rows), F32),
            vmem((2, 8, rows), F32),
            vmem((half, rows), BF16),
            vmem((2, 2, loads, half, rows), BF16),
            vmem((BLOCKS, 2, nz, half, rows), F32),
            vmem((rows // LANE, steps * loads, LANE), F32),
            dma((5,)),
            dma((BLOCKS,)),
            dma((BLOCKS,)),
            dma((BLOCKS,)),
            dma((BLOCKS,)),
            dma((3,)),
            dma((3,)),
            dma((1,)),
            dma((2, loads)),
            dma((2, 2)),
            dma((2,)),
            dma((2, X - 1)),
            dma((BLOCKS,)),
            dma((1 + nz,)),
            dma((BLOCKS,)),
            dma((BLOCKS,)),
            dma((BLOCKS, 2, rows // LANE)),
        ],
        compiler_params=pltpu.CompilerParams(
            collective_id=0, has_side_effects=True, vmem_limit_bytes=60 * 1024 * 1024),
    )(
        lag_offset.reshape(-1), lag_counts.reshape(-1),
        incident, past_density, kernels, couplings, inverse,
    )
    return out.reshape(steps, loads, rows)


def solution(mesh):
    return jax.shard_map(
        functools.partial(local, mesh.shape["src"] // 2),
        mesh=mesh,
        in_specs=(
            P(None, None, "tgt"),
            P(None, None, "src"),
            P(None, "src", "tgt"),
            P("tgt", "src", None),
            P("tgt", "src"),
            P(None, "tgt", None),
            P("tgt", None),
        ),
        out_specs=P(None, None, "tgt"),
        check_vma=False,
    )
```

```python
import functools

import jax
import jax.numpy as jnp
from jax import lax
from jax.experimental import pallas as pl
from jax.experimental.pallas import tpu as pltpu
from jax.sharding import PartitionSpec as P

BLOCKS = 2
LANE = 128
X = 4
MESH = pl.DeviceIdType.MESH
F32 = jnp.float32
BF16 = jnp.bfloat16

C1, C2, INV, A1, A2, Q1, Q2, Q3, D2 = range(9)


def split(value):
    hi = value.astype(BF16)
    return hi, (value - hi.astype(F32)).astype(BF16)


def dot(a, b):
    return jnp.dot(a, b, preferred_element_type=F32)


def dot3(a, b):
    return dot(a[0], b[0]) + dot(a[1], b[0]) + dot(a[0], b[1])


def kernel(
    off_ref, cnt_ref, inc_hbm, past_hbm, ker_hbm, cpl_hbm, inv_hbm, out_hbm,
    inc_v, past_v, ker_v, cpl_v, inv_v, hist, part, abuf, ssum, bsend, brecv,
    tab_hi, tab_lo, mat_hi, mat_lo, pads, shifts, drive, state, tsend, pieces, outbuf, obuf,
    load_sem, a_send, a_recv, b_send, b_recv, st_send, st_recv, t_send, p_recv,
    px_recv, y_send, x_send, o_send, o_recv, f_send, f_recv, out_sem,
    *, nz,
):
    slots, cols, rows = ker_v.shape
    history, loads, _ = past_v.shape
    block = inc_v.shape[0] // BLOCKS
    half = block // 2
    lead = history - block
    hrows = half * loads
    ny = nz
    t = lax.axis_index("tgt")
    s = lax.axis_index("src")
    y, x = t // X, t % X
    z, c = s // 2, s % 2
    oc = 1 - c
    deltas = [(x + X - 2 * c - xs) % X for xs in range(2)]
    member = [delta < 2 for delta in deltas]
    left, right = (x + X - 1) % X, (x + 1) % X
    xs_own = x % 2

    def at(y_, x_, z_, c_):
        return {"tgt": y_ * X + x_, "src": z_ * 2 + c_}

    def remote(src, dst, ssem, rsem, dev):
        return pltpu.make_async_remote_copy(
            src_ref=src, dst_ref=dst, send_sem=ssem, recv_sem=rsem,
            device_id=dev, device_id_type=MESH)

    partner = at(y, x, z, oc)

    past_load = pltpu.make_async_copy(past_hbm, past_v, load_sem.at[0])
    cpl_load = pltpu.make_async_copy(cpl_hbm, cpl_v, load_sem.at[1])
    inv_load = pltpu.make_async_copy(inv_hbm, inv_v, load_sem.at[2])
    inc_load = pltpu.make_async_copy(inc_hbm, inc_v, load_sem.at[3])
    past_load.start()
    for q in range(slots):
        pltpu.make_async_copy(ker_hbm.at[q], ker_v.at[q], load_sem.at[4]).start()
    ker_load = pltpu.make_async_copy(ker_hbm, ker_v, load_sem.at[4])
    for copy in (cpl_load, inv_load, inc_load):
        copy.start()

    barrier = pltpu.get_barrier_semaphore()

    def greet(dev):
        pl.semaphore_signal(barrier, inc=1, device_id=dev, device_id_type=MESH)

    for dz in range(1, nz):
        greet(at(y, x, (z + dz) % nz, c))
    greet(partner)

    for xs in range(2):
        @pl.when(member[xs])
        def _():
            for core in range(2):
                greet(at(z, 2 * c + xs, (2 * z + nz // 2 + nz - y) % nz, core))
            for dy in range(1, ny):
                greet(at((y + dy) % ny, x, z, c))

        @pl.when(deltas[xs] == 2)
        def _():
            greet(at(y, left, z, c))

        @pl.when(deltas[xs] == 3)
        def _():
            greet(at(y, right, z, c))

    hist[0, :, history * loads:, :] = jnp.zeros((cols // LANE, block * loads, LANE), F32)

    past_load.wait()
    @pl.when(t >= 0)
    def _():
        for part_at in range(cols // LANE):
            lanes = slice(part_at * LANE, (part_at + 1) * LANE)
            hist[0, part_at, 0:history * loads, :] = (
                past_v[:, :, lanes].astype(F32).reshape(history * loads, LANE))

    def put(place, value):
        hi, lo = split(value)
        mat_hi[place] = hi
        mat_lo[place] = lo

    def mat(place):
        return mat_hi[place], mat_lo[place]

    cpl_load.wait()
    inv_load.wait()
    put(C1, cpl_v[0])
    put(C2, cpl_v[1])
    put(INV, inv_v[...])
    ker_load.wait()

    def far(blk, h):
        windows = []
        for q in range(slots):
            used = lax.max(lax.min(cnt_ref[0] - q, jnp.int32(1)), jnp.int32(0))
            first = history + used * (lead - history - off_ref[q]) + h * half
            place = pl.ds(first * loads, hrows)
            windows += [hist[blk, k, place, :].astype(BF16) for k in range(cols // LANE)]
        part[blk, pl.ds(pl.multiple_of(h * hrows, hrows), hrows), :] = dot(
            jnp.concatenate(windows, 1), ker_v[...].reshape(slots * cols, rows))

    def far_whole(h):
        @pl.when(t >= 0)
        def _():
            far(1, h)

    held = jnp.logical_and(z == y, c == x // 2)

    def earlier(step):
        both = past_v[step].astype(F32)
        return jnp.where(xs_own == 0, both[:, :rows], both[:, rows:])

    last, before = split(earlier(history - 1)), split(earlier(history - 2))
    first_term = dot3(last, mat(C1)) + dot3(before, mat(C2))
    second_term = dot3(last, mat(C2))

    def far_first(h):
        @pl.when(t >= 0)
        def _():
            far(0, h)

        keep = jnp.where(jnp.logical_and(held, h == 0), 1.0, 0.0).astype(F32)
        base = pl.multiple_of(h * hrows, hrows)
        part[0, pl.ds(base, loads), :] = part[0, pl.ds(base, loads), :] + keep * first_term
        base2 = pl.multiple_of(h * hrows + loads, loads)
        part[0, pl.ds(base2, loads), :] = part[0, pl.ds(base2, loads), :] + keep * second_term

    far_first(oc)

    peers = nz + 2
    for xs in range(2):
        peers = peers + jnp.where(member[xs], ny, 0)
    pl.semaphore_wait(barrier, peers)

    def pair_copy(blk):
        other = pl.ds(pl.multiple_of(oc * hrows, hrows), hrows)
        return remote(part.at[blk, other], abuf.at[blk], a_send.at[blk], a_recv.at[blk], partner)

    pair_copy(0).start()
    far_first(c)

    def ring_send(blk, dz):
        there = (z + dz) % nz
        return remote(bsend.at[blk, there], brecv.at[blk, z], b_send.at[blk], b_recv.at[blk],
                      at(y, x, there, c))

    def ring_all(blk):
        every = pl.ds(0, nz - 1)
        return remote(bsend.at[blk, every], brecv.at[blk, every], b_send.at[blk], b_recv.at[blk],
                      partner)

    far_order = sorted(range(1, nz), key=lambda dz: -min(dz, nz - dz))
    near_order = sorted(range(1, nz), key=lambda dz: min(dz, nz - dz))

    def reduce_start(blk):
        pair_copy(blk).wait_recv()
        mine = pl.ds(pl.multiple_of(c * hrows, hrows), hrows)
        both = part[blk, mine, :] + abuf[blk]
        for k in range(rows // LANE):
            lanes = slice(k * LANE, (k + 1) * LANE)
            ssum[k] = both[:, lanes]
            for load in range(loads):
                bsend[blk, load, :, lanes] = ssum[k, pl.ds(load, half, stride=loads), :]
        for dz in far_order:
            ring_send(blk, dz).start()

    def reduce_finish(blk):
        total = bsend[blk, z]
        ring_all(blk).wait_recv()
        for dz in range(1, nz):
            total = total + brecv[blk, (z + dz) % nz]
        return total

    inc_load.wait()
    row_at = lax.broadcasted_iota(jnp.int32, (half, hrows), 0) * loads + z
    pick = (row_at == lax.broadcasted_iota(jnp.int32, (half, hrows), 1)).astype(BF16)
    for blk in range(BLOCKS):
        steps = inc_v[pl.ds(blk * block + c * half, half)].astype(F32).reshape(hrows, rows)
        drive[blk] = dot(pick, steps.astype(BF16))

    reduce_start(0)

    hist[1, :, history * loads:, :] = jnp.zeros((cols // LANE, block * loads, LANE), F32)
    hist[1, :, 0:lead * loads, :] = hist[0, :, block * loads:history * loads, :]
    pads[:, :half, :] = jnp.zeros((2, half, rows), F32)

    tab_hi[0:rows, :] = jnp.zeros((rows, rows), BF16)
    tab_lo[0:rows, :] = jnp.zeros((rows, rows), BF16)

    def table_put(first, count, value):
        hi, lo = split(value)
        place = pl.ds(pl.multiple_of((first + 1) * rows, rows), count * rows)
        tab_hi[place, :] = hi
        tab_lo[place, :] = lo

    @pl.when(t >= 0)
    def _():
        put(A1, -dot3(mat(C1), mat(INV)))
        put(A2, -dot3(mat(C2), mat(INV)))
        put(Q1, dot3(mat(A1), mat(A1)) + (mat_hi[A2].astype(F32) + mat_lo[A2].astype(F32)))
        put(Q2, dot3(mat(Q1), mat(A1)) + dot3(mat(A1), mat(A2)))
        put(Q3, dot3(mat(Q2), mat(A1)) + dot3(mat(Q1), mat(A2)))
        put(D2, dot3(mat(A2), mat(Q2)))
        table_put(0, 1, inv_v[...])
        table_put(1, 1, dot3(mat(INV), mat(A1)))
        table_put(2, 1, dot3(mat(INV), mat(Q1)))
        table_put(3, 1, dot3(mat(INV), mat(Q2)))

    def four_more(step, carry):
        one = pl.ds(pl.multiple_of((4 * step - 3) * rows, rows), 4 * rows)
        two = pl.ds(pl.multiple_of((4 * step - 4) * rows, rows), 4 * rows)
        value = dot3((tab_hi[one, :], tab_lo[one, :]), mat(Q3))
        value = value + dot3((tab_hi[two, :], tab_lo[two, :]), mat(D2))
        table_put(4 * step, 4, value)
        return carry

    @pl.when(t >= 0)
    def _():
        lax.fori_loop(1, half // 4, four_more, 0)

    def state_copy(which):
        blk = which // 2
        held_by = which % 2
        return remote(outbuf.at[blk, c, z, pl.ds(half - 8, 8)], state.at[(which + 1) // 2],
                      st_send.at[which], st_recv.at[which], partner), held_by

    def state_start(which):
        copy, held_by = state_copy(which)

        @pl.when(c == held_by)
        def _():
            copy.start()

    def state_wait(which):
        copy, held_by = state_copy(which)

        @pl.when(c != held_by)
        def _():
            copy.wait_recv()

    def state_sent(which):
        copy, held_by = state_copy(which)

        @pl.when(c == held_by)
        def _():
            copy.wait_send()

    def respond(blk, from_state):
        from_state = split(from_state)
        by_one, by_two = dot3(from_state, mat(C1)), dot3(from_state, mat(C2))
        row = lax.broadcasted_iota(jnp.int32, by_one.shape, 0)
        change = jnp.where(row == 0, pltpu.roll(by_one, 1, 0), 0.0)
        change = change + jnp.where(row < 2, pltpu.roll(by_two, 2, 0), 0.0)
        drive[blk, 0:8] = drive[blk, 0:8] - change
        hi, lo = split(drive[blk])
        pads[0, half:, :] = hi.astype(F32)
        pads[1, half:, :] = lo.astype(F32)
        for k in range(half):
            there = slice(k * rows, (k + 1) * rows)
            shifts[0:half, there] = pads[0, half - k:2 * half - k, :].astype(BF16)
            shifts[half:, there] = pads[1, half - k:2 * half - k, :].astype(BF16)
        both = dot(shifts[...], tab_hi[rows:, :])
        outbuf[blk, c, z] = both[:half] + both[half:] + dot(shifts[0:half, :], tab_lo[rows:, :])

    drive[0] = drive[0] - reduce_finish(0)

    @pl.when(c == 0)
    def _():
        respond(0, jnp.zeros((8, rows), F32))

    @pl.when(c == 1)
    def _():
        state_wait(0)
        respond(0, state[0])

    state_start(0)
    state_start(1)

    def turn_copy(column):
        return remote(tsend, pieces.at[c, xs_own, z], t_send.at[column], p_recv.at[c, xs_own, z],
                      at((2 * y + nz // 2 + nz - z) % ny, (x + column) % X, y, x // 2))

    tsend[...] = outbuf[0, c, z].astype(BF16)
    for column in (1, 0):
        turn_copy(column).start()

    def load_of(y_):
        return (2 * z + nz // 2 + nz - y_) % nz

    def arrived(h, xs, load):
        ref = pieces.at[h, xs, load]
        remote(ref, ref, t_send.at[0], p_recv.at[h, xs, load], partner).wait_recv()

    def along_y(h, xs, dy):
        load = load_of(y)
        ref = pieces.at[h, xs, load]
        return remote(ref, ref, y_send.at[h, xs], p_recv.at[h, xs, load],
                      at((y + dy) % ny, x, z, c))

    def along_x(h, xs, dy):
        ref = pieces.at[h, xs, load_of((y + ny - dy) % ny)]
        to = jnp.where(deltas[xs] == 0, left, right)
        return remote(ref, ref, x_send.at[h, xs], px_recv.at[h, xs], at(y, to, z, c))

    def all_x(h, xs):
        ref = pieces.at[h, xs]
        return remote(ref, ref, x_send.at[h, xs], px_recv.at[h, xs], partner)

    def handed_on(h):
        for xs in range(2):
            @pl.when(member[xs])
            def _():
                some = pieces.at[h, xs, pl.ds(0, ny - 1)]
                remote(some, some, y_send.at[h, xs], p_recv.at[h, xs, 0], partner).wait_send()
                all_x(h, xs).wait_send()

    def hand_on(h):
        for xs in range(2):
            @pl.when(member[xs])
            def _():
                arrived(h, xs, load_of(y))
                for dy in far_order:
                    along_y(h, xs, dy).start()
                along_x(h, xs, 0).start()
        for dy in near_order:
            for xs in range(2):
                @pl.when(member[xs])
                def _():
                    arrived(h, xs, load_of((y + ny - dy) % ny))
                    along_x(h, xs, dy).start()

    def take_in(h):
        for xs in range(2):
            @pl.when(jnp.logical_not(member[xs]))
            def _():
                all_x(h, xs).wait_recv()
        for xs in range(2):
            for load in range(loads):
                to = pl.ds((lead + h * half) * loads + load, half, stride=loads)
                for k in range(rows // LANE):
                    part_of = pieces[h, xs, load, :, k * LANE:(k + 1) * LANE]
                    hist[1, xs * (rows // LANE) + k, to, :] = part_of.astype(F32)

    def direct_sem(blk, from_z):
        return o_recv.at[0] if blk == 0 else o_recv.at[1 + from_z]

    def own_copy(blk, dz):
        ref = outbuf.at[blk, c, z]
        there = (z + dz) % nz
        return remote(ref, ref, o_send.at[blk], direct_sem(blk, z), at(y, x, there, c))

    def own_all(blk):
        some = outbuf.at[blk, c, pl.ds(0, nz - 1)]
        return remote(some, some, o_send.at[blk], o_recv.at[0], partner)

    def own_arrival(blk, from_z):
        ref = outbuf.at[blk, c, from_z]
        remote(ref, ref, o_send.at[blk], direct_sem(blk, from_z), partner).wait_recv()

    def cross_copy(blk, from_z):
        ref = outbuf.at[blk, c, from_z]
        return remote(ref, ref, f_send.at[blk], f_recv.at[blk], partner)

    def cross_all(blk, h):
        ref = outbuf.at[blk, h]
        return remote(ref, ref, f_send.at[blk], f_recv.at[blk], partner)

    def spread_start(blk):
        for dz in far_order:
            own_copy(blk, dz).start()
        cross_copy(blk, z).start()

    def spread_cross(blk):
        if blk == 0:
            own_all(blk).wait_recv()
        for dz in near_order:
            from_z = (z + nz - dz) % nz
            if blk == 1:
                own_arrival(blk, from_z)
            cross_copy(blk, from_z).start()

    def spread_sent(blk):
        own_all(blk).wait_send()
        cross_all(blk, 0).wait_send()

    def out_copy(blk, h, k):
        first = pl.multiple_of((blk * block + h * half) * loads, loads)
        place = pl.ds(first, hrows)
        return pltpu.make_async_copy(
            obuf.at[k, place], out_hbm.at[place, pl.ds(k * LANE, LANE)], out_sem.at[blk, h, k])

    def out_start(blk, h):
        for k in range(rows // LANE):
            for load in range(loads):
                to = pl.ds((blk * block + h * half) * loads + load, half, stride=loads)
                obuf[k, to, :] = outbuf[blk, h, load, :, k * LANE:(k + 1) * LANE]
            out_copy(blk, h, k).start()

    hand_on(0)
    hand_on(1)
    spread_start(0)
    take_in(0)
    far_whole(0)

    @pl.when(c == 1)
    def _():
        pair_copy(1).start()

    @pl.when(c == 0)
    def _():
        reduce_start(1)

    take_in(1)
    far_whole(1)

    @pl.when(c == 0)
    def _():
        pair_copy(1).start()

    @pl.when(c == 1)
    def _():
        reduce_start(1)

    spread_cross(0)
    ring_all(0).wait_send()
    for blk in range(BLOCKS):
        pair_copy(blk).wait_send()
    for column in range(2):
        turn_copy(column).wait_send()
    for which in range(2):
        state_sent(which)

    for h in range(2):
        handed_on(h)

    drive[1] = drive[1] - reduce_finish(1)
    state_wait(1)
    state_wait(2)

    @pl.when(t >= 0)
    def _():
        respond(1, state[1])

    spread_start(1)
    state_start(2)

    cross_all(0, oc).wait_recv()
    spread_sent(0)
    ring_all(1).wait_send()
    for h in range(2):
        out_start(0, h)
    state_sent(2)

    spread_cross(1)

    @pl.when(c == 1)
    def _():
        cross_all(1, 0).wait_recv()
        out_start(1, 0)
        out_start(1, 1)

    @pl.when(c == 0)
    def _():
        out_start(1, 0)
        cross_all(1, 1).wait_recv()
        out_start(1, 1)

    spread_sent(1)
    for k in range(rows // LANE):
        for blk in range(BLOCKS):
            for h in range(2):
                out_copy(blk, h, k).wait()


def local(nz, incident, past_density, kernels, lag_offset, lag_counts, couplings, inverse):
    steps, loads, rows = incident.shape
    history, _, cols = past_density.shape
    slots = kernels.shape[0]
    block = steps // BLOCKS
    half = block // 2
    hrows = half * loads
    vmem = pltpu.VMEM
    dma = pltpu.SemaphoreType.DMA
    out = pl.pallas_call(
        functools.partial(kernel, nz=nz),
        out_shape=jax.ShapeDtypeStruct((steps * loads, rows), F32),
        in_specs=[pl.BlockSpec(memory_space=pltpu.SMEM)] * 2
        + [pl.BlockSpec(memory_space=pl.ANY)] * 5,
        out_specs=pl.BlockSpec(memory_space=pl.ANY),
        scratch_shapes=[
            vmem((steps, loads, rows), BF16),
            vmem((history, loads, cols), BF16),
            vmem((slots, cols, rows), BF16),
            vmem((2, rows, rows), F32),
            vmem((rows, rows), F32),
            vmem((BLOCKS, cols // LANE, (history + block) * loads, LANE), F32),
            vmem((BLOCKS, block * loads, rows), F32),
            vmem((BLOCKS, hrows, rows), F32),
            vmem((rows // LANE, hrows, LANE), F32),
            vmem((BLOCKS, nz, half, rows), F32),
            vmem((BLOCKS, nz, half, rows), F32),
            vmem(((half + 1) * rows, rows), BF16),
            vmem(((half + 1) * rows, rows), BF16),
            vmem((9, rows, rows), BF16),
            vmem((9, rows, rows), BF16),
            vmem((2, 2 * half, rows), F32),
            vmem((2 * half, half * rows), BF16),
            vmem((BLOCKS, half, rows), F32),
            vmem((2, 8, rows), F32),
            vmem((half, rows), BF16),
            vmem((2, 2, loads, half, rows), BF16),
            vmem((BLOCKS, 2, nz, half, rows), F32),
            vmem((rows // LANE, steps * loads, LANE), F32),
            dma((5,)),
            dma((BLOCKS,)),
            dma((BLOCKS,)),
            dma((BLOCKS,)),
            dma((BLOCKS,)),
            dma((3,)),
            dma((3,)),
            dma((2,)),
            dma((2, 2, loads)),
            dma((2, 2)),
            dma((2, 2)),
            dma((2, 2)),
            dma((BLOCKS,)),
            dma((1 + nz,)),
            dma((BLOCKS,)),
            dma((BLOCKS,)),
            dma((BLOCKS, 2, rows // LANE)),
        ],
        compiler_params=pltpu.CompilerParams(
            collective_id=0, has_side_effects=True, vmem_limit_bytes=60 * 1024 * 1024),
    )(
        lag_offset.reshape(-1), lag_counts.reshape(-1),
        incident, past_density, kernels, couplings, inverse,
    )
    return out.reshape(steps, loads, rows)


def solution(mesh):
    return jax.shard_map(
        functools.partial(local, mesh.shape["src"] // 2),
        mesh=mesh,
        in_specs=(
            P(None, None, "tgt"),
            P(None, None, "src"),
            P(None, "src", "tgt"),
            P("tgt", "src", None),
            P("tgt", "src"),
            P(None, "tgt", None),
            P("tgt", None),
        ),
        out_specs=P(None, None, "tgt"),
        check_vma=False,
    )
```

```python
import functools

import jax
import jax.numpy as jnp
from jax import lax
from jax.experimental import pallas as pl
from jax.experimental.pallas import tpu as pltpu
from jax.sharding import PartitionSpec as P

BLOCKS = 2
LANE = 128
X = 4
MESH = pl.DeviceIdType.MESH
F32 = jnp.float32
BF16 = jnp.bfloat16

C1, C2, INV, A1, A2, Q1, Q2, Q3, D2 = range(9)


def split(value):
    hi = value.astype(BF16)
    return hi, (value - hi.astype(F32)).astype(BF16)


def dot(a, b):
    return jnp.dot(a, b, preferred_element_type=F32)


def dot3(a, b):
    return dot(a[0], b[0]) + dot(a[1], b[0]) + dot(a[0], b[1])


def kernel(
    off_ref, cnt_ref, inc_hbm, past_hbm, ker_hbm, cpl_hbm, inv_hbm, out_hbm,
    inc_v, past_v, ker_v, cpl_v, inv_v, hist, part, abuf, ssum, bsend, brecv,
    terms, tab_hi, tab_lo, mat_hi, mat_lo, pads, shifts, drive, state, tsend, pieces, outbuf, obuf,
    load_sem, a_send, a_recv, b_send, b_recv, st_send, st_recv, t_send, p_recv,
    px_recv, y_send, x_send, o_send, o_recv, f_send, f_recv, out_sem,
    *, nz,
):
    slots, cols, rows = ker_v.shape
    history, loads, _ = past_v.shape
    block = inc_v.shape[0] // BLOCKS
    half = block // 2
    lead = history - block
    hrows = half * loads
    ny = nz
    t = lax.axis_index("tgt")
    s = lax.axis_index("src")
    y, x = t // X, t % X
    z, c = s // 2, s % 2
    oc = 1 - c
    member = c == x // 2
    xs_own = x % 2

    def at(y_, x_, z_, c_):
        return {"tgt": y_ * X + x_, "src": z_ * 2 + c_}

    def remote(src, dst, ssem, rsem, dev):
        return pltpu.make_async_remote_copy(
            src_ref=src, dst_ref=dst, send_sem=ssem, recv_sem=rsem,
            device_id=dev, device_id_type=MESH)

    partner = at(y, x, z, oc)

    past_load = pltpu.make_async_copy(past_hbm, past_v, load_sem.at[0])
    cpl_load = pltpu.make_async_copy(cpl_hbm, cpl_v, load_sem.at[1])
    inv_load = pltpu.make_async_copy(inv_hbm, inv_v, load_sem.at[2])
    inc_load = pltpu.make_async_copy(inc_hbm, inc_v, load_sem.at[3])
    past_load.start()
    for q in range(slots):
        pltpu.make_async_copy(ker_hbm.at[q], ker_v.at[q], load_sem.at[4]).start()
    ker_load = pltpu.make_async_copy(ker_hbm, ker_v, load_sem.at[4])
    for copy in (cpl_load, inv_load, inc_load):
        copy.start()

    barrier = pltpu.get_barrier_semaphore()

    def greet(dev):
        pl.semaphore_signal(barrier, inc=1, device_id=dev, device_id_type=MESH)

    for dz in range(1, nz):
        greet(at(y, x, (z + dz) % nz, c))
    greet(partner)

    @pl.when(member)
    def _():
        for core in range(2):
            greet(at(z, x, (2 * z + nz // 2 + nz - y) % nz, core))
        for dy in range(1, ny):
            greet(at((y + dy) % ny, x, z, c))

    for xs in range(2):
        @pl.when(2 * c + xs != x)
        def _():
            greet(at(y, 2 * c + xs, z, c))

    hist[0, :, history * loads:, :] = jnp.zeros((cols // LANE, block * loads, LANE), F32)

    past_load.wait()
    @pl.when(t >= 0)
    def _():
        for part_at in range(cols // LANE):
            lanes = slice(part_at * LANE, (part_at + 1) * LANE)
            hist[0, part_at, 0:history * loads, :] = (
                past_v[:, :, lanes].astype(F32).reshape(history * loads, LANE))

    def put(place, value):
        hi, lo = split(value)
        mat_hi[place] = hi
        mat_lo[place] = lo

    def mat(place):
        return mat_hi[place], mat_lo[place]

    ker_load.wait()

    def far(blk, h):
        windows = []
        for q in range(slots):
            used = lax.max(lax.min(cnt_ref[0] - q, jnp.int32(1)), jnp.int32(0))
            first = history + used * (lead - history - off_ref[q]) + h * half
            place = pl.ds(first * loads, hrows)
            windows += [hist[blk, k, place, :].astype(BF16) for k in range(cols // LANE)]
        part[blk, pl.ds(pl.multiple_of(h * hrows, hrows), hrows), :] = dot(
            jnp.concatenate(windows, 1), ker_v[...].reshape(slots * cols, rows))

    def far_whole(h):
        @pl.when(t >= 0)
        def _():
            far(1, h)

    held = jnp.logical_and(z == y, member)

    def earlier(step):
        both = past_v[step].astype(F32)
        return jnp.where(xs_own == 0, both[:, :rows], both[:, rows:])

    def far_first(h):
        @pl.when(t >= 0)
        def _():
            far(0, h)

    def state_first(h):
        keep = jnp.where(jnp.logical_and(held, h == 0), 1.0, 0.0).astype(F32)
        base = pl.multiple_of(h * hrows, hrows)
        part[0, pl.ds(base, loads), :] = part[0, pl.ds(base, loads), :] + keep * terms[0:loads]
        base2 = pl.multiple_of(h * hrows + loads, loads)
        part[0, pl.ds(base2, loads), :] = part[0, pl.ds(base2, loads), :] + keep * terms[loads:]

    far_first(oc)
    cpl_load.wait()

    @pl.when(t >= 0)
    def _():
        put(C1, cpl_v[0])
        put(C2, cpl_v[1])
        last, before = split(earlier(history - 1)), split(earlier(history - 2))
        terms[0:loads] = dot3(last, mat(C1)) + dot3(before, mat(C2))
        terms[loads:] = dot3(last, mat(C2))

    state_first(oc)

    @pl.when(member)
    def _():
        pl.semaphore_wait(barrier, nz + 1 + ny - 1 + X - 1)

    @pl.when(jnp.logical_not(member))
    def _():
        pl.semaphore_wait(barrier, nz + 1)

    def pair_copy(blk):
        other = pl.ds(pl.multiple_of(oc * hrows, hrows), hrows)
        return remote(part.at[blk, other], abuf.at[blk], a_send.at[blk], a_recv.at[blk], partner)

    pair_copy(0).start()
    far_first(c)
    state_first(c)

    def ring_send(blk, dz):
        there = (z + dz) % nz
        return remote(bsend.at[blk, there], brecv.at[blk, z], b_send.at[blk], b_recv.at[blk],
                      at(y, x, there, c))

    def ring_all(blk):
        every = pl.ds(0, nz - 1)
        return remote(bsend.at[blk, every], brecv.at[blk, every], b_send.at[blk], b_recv.at[blk],
                      partner)

    far_order = sorted(range(1, nz), key=lambda dz: -min(dz, nz - dz))
    near_order = sorted(range(1, nz), key=lambda dz: min(dz, nz - dz))

    def reduce_start(blk):
        pair_copy(blk).wait_recv()
        mine = pl.ds(pl.multiple_of(c * hrows, hrows), hrows)
        both = part[blk, mine, :] + abuf[blk]
        for k in range(rows // LANE):
            lanes = slice(k * LANE, (k + 1) * LANE)
            ssum[k] = both[:, lanes]
            for load in range(loads):
                bsend[blk, load, :, lanes] = ssum[k, pl.ds(load, half, stride=loads), :]
        for dz in far_order:
            ring_send(blk, dz).start()

    def reduce_finish(blk):
        total = bsend[blk, z]
        ring_all(blk).wait_recv()
        for dz in range(1, nz):
            total = total + brecv[blk, (z + dz) % nz]
        return total

    reduce_start(0)

    inc_load.wait()
    row_at = lax.broadcasted_iota(jnp.int32, (half, hrows), 0) * loads + z
    pick = (row_at == lax.broadcasted_iota(jnp.int32, (half, hrows), 1)).astype(BF16)
    for blk in range(BLOCKS):
        steps = inc_v[pl.ds(blk * block + c * half, half)].astype(F32).reshape(hrows, rows)
        drive[blk] = dot(pick, steps.astype(BF16))


    hist[1, :, history * loads:, :] = jnp.zeros((cols // LANE, block * loads, LANE), F32)
    hist[1, :, 0:lead * loads, :] = hist[0, :, block * loads:history * loads, :]
    pads[:, :half, :] = jnp.zeros((2, half, rows), F32)

    inv_load.wait()
    put(INV, inv_v[...])
    tab_hi[0:rows, :] = jnp.zeros((rows, rows), BF16)
    tab_lo[0:rows, :] = jnp.zeros((rows, rows), BF16)

    def table_put(first, count, value):
        hi, lo = split(value)
        place = pl.ds(pl.multiple_of((first + 1) * rows, rows), count * rows)
        tab_hi[place, :] = hi
        tab_lo[place, :] = lo

    @pl.when(t >= 0)
    def _():
        put(A1, -dot3(mat(C1), mat(INV)))
        put(A2, -dot3(mat(C2), mat(INV)))
        put(Q1, dot3(mat(A1), mat(A1)) + (mat_hi[A2].astype(F32) + mat_lo[A2].astype(F32)))
        put(Q2, dot3(mat(Q1), mat(A1)) + dot3(mat(A1), mat(A2)))
        put(Q3, dot3(mat(Q2), mat(A1)) + dot3(mat(Q1), mat(A2)))
        put(D2, dot3(mat(A2), mat(Q2)))
        table_put(0, 1, inv_v[...])
        table_put(1, 1, dot3(mat(INV), mat(A1)))
        table_put(2, 1, dot3(mat(INV), mat(Q1)))
        table_put(3, 1, dot3(mat(INV), mat(Q2)))

    def four_more(step, carry):
        one = pl.ds(pl.multiple_of((4 * step - 3) * rows, rows), 4 * rows)
        two = pl.ds(pl.multiple_of((4 * step - 4) * rows, rows), 4 * rows)
        value = dot3((tab_hi[one, :], tab_lo[one, :]), mat(Q3))
        value = value + dot3((tab_hi[two, :], tab_lo[two, :]), mat(D2))
        table_put(4 * step, 4, value)
        return carry

    @pl.when(t >= 0)
    def _():
        lax.fori_loop(1, half // 4, four_more, 0)

    def state_copy(which):
        blk = which // 2
        held_by = which % 2
        return remote(outbuf.at[blk, c, z, pl.ds(half - 8, 8)], state.at[(which + 1) // 2],
                      st_send.at[which], st_recv.at[which], partner), held_by

    def state_start(which):
        copy, held_by = state_copy(which)

        @pl.when(c == held_by)
        def _():
            copy.start()

    def state_wait(which):
        copy, held_by = state_copy(which)

        @pl.when(c != held_by)
        def _():
            copy.wait_recv()

    def state_sent(which):
        copy, held_by = state_copy(which)

        @pl.when(c == held_by)
        def _():
            copy.wait_send()

    def respond(blk, from_state):
        from_state = split(from_state)
        by_one, by_two = dot3(from_state, mat(C1)), dot3(from_state, mat(C2))
        row = lax.broadcasted_iota(jnp.int32, by_one.shape, 0)
        change = jnp.where(row == 0, pltpu.roll(by_one, 1, 0), 0.0)
        change = change + jnp.where(row < 2, pltpu.roll(by_two, 2, 0), 0.0)
        drive[blk, 0:8] = drive[blk, 0:8] - change
        hi, lo = split(drive[blk])
        pads[0, half:, :] = hi.astype(F32)
        pads[1, half:, :] = lo.astype(F32)
        for k in range(half):
            there = slice(k * rows, (k + 1) * rows)
            shifts[0:half, there] = pads[0, half - k:2 * half - k, :].astype(BF16)
            shifts[half:, there] = pads[1, half - k:2 * half - k, :].astype(BF16)
        both = dot(shifts[...], tab_hi[rows:, :])
        outbuf[blk, c, z] = both[:half] + both[half:] + dot(shifts[0:half, :], tab_lo[rows:, :])

    drive[0] = drive[0] - reduce_finish(0)

    @pl.when(c == 0)
    def _():
        respond(0, jnp.zeros((8, rows), F32))

    @pl.when(c == 1)
    def _():
        state_wait(0)
        respond(0, state[0])

    state_start(0)
    state_start(1)

    def turn_copy():
        dst = pieces.at[c, xs_own, 0]
        return remote(tsend, dst, t_send.at[0], p_recv.at[c, 0],
                      at((2 * y + nz // 2 + nz - z) % ny, x, y, x // 2))

    tsend[...] = outbuf[0, c, z].astype(BF16)
    turn_copy().start()

    def load_of(y_):
        return (2 * z + nz // 2 + nz - y_) % nz

    y_order = [0] + near_order

    def arrived(h, slot):
        ref = pieces.at[h, xs_own, slot]
        remote(ref, ref, t_send.at[0], p_recv.at[h, slot], partner).wait_recv()

    def along_y(h, dy):
        slot = y_order.index(dy)
        return remote(pieces.at[h, xs_own, 0], pieces.at[h, xs_own, slot], y_send.at[h],
                      p_recv.at[h, slot], at((y + dy) % ny, x, z, c))

    def along_x(h, first, count, dx):
        ref = pieces.at[h, xs_own, pl.ds(first, count)]
        return remote(ref, ref, x_send.at[h, dx - 1], px_recv.at[h, xs_own],
                      at(y, (x + dx) % X, z, c))

    def all_x(h, xs, dx):
        ref = pieces.at[h, xs]
        return remote(ref, ref, x_send.at[h, dx - 1], px_recv.at[h, xs], partner)

    def handed_on(h):
        some = pieces.at[h, 0, pl.ds(0, ny - 1)]
        remote(some, some, y_send.at[h], p_recv.at[h, 0], partner).wait_send()
        for dx in range(1, X):
            all_x(h, 0, dx).wait_send()

    def hand_on(h):
        @pl.when(member)
        def _():
            arrived(h, 0)
            for dy in far_order:
                along_y(h, dy).start()
            first = 0
            for slot in range(ny):
                if slot > 0:
                    arrived(h, slot)
                if slot % 2 == 1:
                    for dx in (2, 1, 3):
                        along_x(h, first, slot + 1 - first, dx).start()
                    first = slot + 1

    def take_in(h):
        for xs in range(2):
            @pl.when(2 * c + xs != x)
            def _():
                all_x(h, xs, 1).wait_recv()
        for xs in range(2):
            for load in range(loads):
                dy = (load + nz - load_of(y)) % nz
                slot = jnp.where(dy > ny // 2, 2 * (ny - dy), jnp.maximum(2 * dy - 1, 0))
                to = pl.ds((lead + h * half) * loads + load, half, stride=loads)
                for k in range(rows // LANE):
                    part_of = pieces[h, xs, slot, :, k * LANE:(k + 1) * LANE]
                    hist[1, xs * (rows // LANE) + k, to, :] = part_of.astype(F32)

    def direct_sem(blk, from_z):
        return o_recv.at[0] if blk == 0 else o_recv.at[1 + from_z]

    def own_copy(blk, dz):
        ref = outbuf.at[blk, c, z]
        there = (z + dz) % nz
        return remote(ref, ref, o_send.at[blk], direct_sem(blk, z), at(y, x, there, c))

    def own_all(blk):
        some = outbuf.at[blk, c, pl.ds(0, nz - 1)]
        return remote(some, some, o_send.at[blk], o_recv.at[0], partner)

    def own_arrival(blk, from_z):
        ref = outbuf.at[blk, c, from_z]
        remote(ref, ref, o_send.at[blk], direct_sem(blk, from_z), partner).wait_recv()

    def cross_copy(blk, from_z):
        ref = outbuf.at[blk, c, from_z]
        return remote(ref, ref, f_send.at[blk], f_recv.at[blk], partner)

    def cross_all(blk, h):
        ref = outbuf.at[blk, h]
        return remote(ref, ref, f_send.at[blk], f_recv.at[blk], partner)

    def spread_start(blk):
        for dz in far_order:
            own_copy(blk, dz).start()
        cross_copy(blk, z).start()

    def spread_cross(blk):
        if blk == 0:
            own_all(blk).wait_recv()
        for dz in near_order:
            from_z = (z + nz - dz) % nz
            if blk == 1:
                own_arrival(blk, from_z)
            cross_copy(blk, from_z).start()

    def spread_sent(blk):
        own_all(blk).wait_send()
        cross_all(blk, 0).wait_send()

    def out_copy(blk, h, k):
        first = pl.multiple_of((blk * block + h * half) * loads, loads)
        place = pl.ds(first, hrows)
        return pltpu.make_async_copy(
            obuf.at[k, place], out_hbm.at[place, pl.ds(k * LANE, LANE)], out_sem.at[blk, h, k])

    def out_start(blk, h):
        for k in range(rows // LANE):
            for load in range(loads):
                to = pl.ds((blk * block + h * half) * loads + load, half, stride=loads)
                obuf[k, to, :] = outbuf[blk, h, load, :, k * LANE:(k + 1) * LANE]
            out_copy(blk, h, k).start()

    hand_on(0)
    hand_on(1)
    spread_start(0)
    take_in(0)
    far_whole(0)

    @pl.when(c == 1)
    def _():
        pair_copy(1).start()

    @pl.when(c == 0)
    def _():
        reduce_start(1)

    take_in(1)
    far_whole(1)

    @pl.when(c == 0)
    def _():
        pair_copy(1).start()

    @pl.when(c == 1)
    def _():
        reduce_start(1)

    spread_cross(0)
    ring_all(0).wait_send()
    for blk in range(BLOCKS):
        pair_copy(blk).wait_send()
    turn_copy().wait_send()
    for which in range(2):
        state_sent(which)

    @pl.when(member)
    def _():
        for h in range(2):
            handed_on(h)

    drive[1] = drive[1] - reduce_finish(1)
    state_wait(1)
    state_wait(2)

    @pl.when(t >= 0)
    def _():
        respond(1, state[1])

    spread_start(1)
    state_start(2)

    cross_all(0, oc).wait_recv()
    spread_sent(0)
    ring_all(1).wait_send()
    for h in range(2):
        out_start(0, h)
    state_sent(2)

    spread_cross(1)

    @pl.when(c == 1)
    def _():
        cross_all(1, 0).wait_recv()
        out_start(1, 0)
        out_start(1, 1)

    @pl.when(c == 0)
    def _():
        out_start(1, 0)
        cross_all(1, 1).wait_recv()
        out_start(1, 1)

    spread_sent(1)
    for k in range(rows // LANE):
        for blk in range(BLOCKS):
            for h in range(2):
                out_copy(blk, h, k).wait()


def local(nz, incident, past_density, kernels, lag_offset, lag_counts, couplings, inverse):
    steps, loads, rows = incident.shape
    history, _, cols = past_density.shape
    slots = kernels.shape[0]
    block = steps // BLOCKS
    half = block // 2
    hrows = half * loads
    vmem = pltpu.VMEM
    dma = pltpu.SemaphoreType.DMA
    out = pl.pallas_call(
        functools.partial(kernel, nz=nz),
        out_shape=jax.ShapeDtypeStruct((steps * loads, rows), F32),
        in_specs=[pl.BlockSpec(memory_space=pltpu.SMEM)] * 2
        + [pl.BlockSpec(memory_space=pl.ANY)] * 5,
        out_specs=pl.BlockSpec(memory_space=pl.ANY),
        scratch_shapes=[
            vmem((steps, loads, rows), BF16),
            vmem((history, loads, cols), BF16),
            vmem((slots, cols, rows), BF16),
            vmem((2, rows, rows), F32),
            vmem((rows, rows), F32),
            vmem((BLOCKS, cols // LANE, (history + block) * loads, LANE), F32),
            vmem((BLOCKS, block * loads, rows), F32),
            vmem((BLOCKS, hrows, rows), F32),
            vmem((rows // LANE, hrows, LANE), F32),
            vmem((BLOCKS, nz, half, rows), F32),
            vmem((BLOCKS, nz, half, rows), F32),
            vmem((2 * loads, rows), F32),
            vmem(((half + 1) * rows, rows), BF16),
            vmem(((half + 1) * rows, rows), BF16),
            vmem((9, rows, rows), BF16),
            vmem((9, rows, rows), BF16),
            vmem((2, 2 * half, rows), F32),
            vmem((2 * half, half * rows), BF16),
            vmem((BLOCKS, half, rows), F32),
            vmem((2, 8, rows), F32),
            vmem((half, rows), BF16),
            vmem((2, 2, loads, half, rows), BF16),
            vmem((BLOCKS, 2, nz, half, rows), F32),
            vmem((rows // LANE, steps * loads, LANE), F32),
            dma((5,)),
            dma((BLOCKS,)),
            dma((BLOCKS,)),
            dma((BLOCKS,)),
            dma((BLOCKS,)),
            dma((3,)),
            dma((3,)),
            dma((1,)),
            dma((2, loads)),
            dma((2, 2)),
            dma((2,)),
            dma((2, X - 1)),
            dma((BLOCKS,)),
            dma((1 + nz,)),
            dma((BLOCKS,)),
            dma((BLOCKS,)),
            dma((BLOCKS, 2, rows // LANE)),
        ],
        compiler_params=pltpu.CompilerParams(
            collective_id=0, has_side_effects=True, vmem_limit_bytes=60 * 1024 * 1024),
    )(
        lag_offset.reshape(-1), lag_counts.reshape(-1),
        incident, past_density, kernels, couplings, inverse,
    )
    return out.reshape(steps, loads, rows)


def solution(mesh):
    return jax.shard_map(
        functools.partial(local, mesh.shape["src"] // 2),
        mesh=mesh,
        in_specs=(
            P(None, None, "tgt"),
            P(None, None, "src"),
            P(None, "src", "tgt"),
            P("tgt", "src", None),
            P("tgt", "src"),
            P(None, "tgt", None),
            P("tgt", None),
        ),
        out_specs=P(None, None, "tgt"),
        check_vma=False,
    )
```
